256 devices in a mesh: alpha: 4 (over x), beta: 64 (over z, y, core).
Axes of the slice: x: 4, y: 4, z: 8, core: 2. Of those that a mesh axis runs over, the one named last changes fastest.
Arguments:
- civec: float32 [1024, 24576], P('alpha', 'beta'), may hold values from -6 to 6
- batch_index: int32 [8], replicated, may hold values from 0 to 1023, as said below
- exc_alpha: int32 [3, 8, 81], replicated, may hold values from -1 to 1023, as said below
- exc_beta: int32 [3, 24576, 81], P(None, 'beta'), may hold values from -1 to 24575, as said below
- one_body: float32 [324], replicated, may hold values from -0.625 to 0.625
Outputs:
- sigma: float32 [8, 24576], P('alpha', 'beta')
- density_one: float32 [2, 324], replicated
- rdm_same: float32 [324, 324], replicated
- rdm_mixed: float32 [324, 324], replicated
The draws below stay inside these ranges and needn't reach their ends.
Inputs may be any that keep to these rules, and one draw needn't show every extreme that they name: `batch_index`: entries b * 2 to (b + 1) * 2 - 1 for b = 0..3 are distinct strings of the block b * 256 to (b + 1) * 256 - 1. `exc_alpha`: plane 0 holds source alpha strings below 1024, plane 1 pair indices below 324, distinct within each row, plane 2 signs -1, 0 or 1; a slot with sign 0 is empty, live slots come first, every row has at least 40 live slots and some row has all 81. `exc_beta`: plane 0 holds source beta strings below 24576, plane 1 pair indices below 324, distinct within each row, plane 2 signs -1, 0 or 1; a slot with sign 0 is empty, live slots come first, every row has at least 40 live slots and some row has all 81.
All inputs are finite; a program needn't handle non-finite values.
Results may differ from the reference program's by a relative error of at most 0.0003.
Values sent between devices are 32-bit elements; how exact they have to be, the bound alone decides.
A program may use at most 192 MiB of HBM per device.

```python
import math
import jax
import jax.numpy as jnp
from jax import lax

PAIRS = 324
NEXC = 81
ROWS_DEV = 256
NA = 1024
NBETA = 24576
BATCH = 2
NB = 8


def make_lists(key, rows, span):
    count_key, pair_key, source_key, sign_key = jax.random.split(key, 4)
    counts = jax.random.randint(count_key, (rows,), NEXC // 2, NEXC + 1)
    counts = counts.at[0].set(NEXC)
    scores = jax.random.randint(pair_key, (rows, PAIRS), 0, 1 << 20) * PAIRS + jnp.arange(PAIRS)[None, :]
    pair_ids = jnp.argsort(scores, axis=1)[:, :NEXC].astype(jnp.int32)
    pair_ids = pair_ids.at[0].set((PAIRS - 1 - jnp.arange(NEXC)).astype(jnp.int32))
    sources = jax.random.randint(source_key, (rows, NEXC), 0, span)
    signs = 2 * jax.random.randint(sign_key, (rows, NEXC), 0, 2) - 1
    live = jnp.arange(NEXC)[None, :] < counts[:, None]
    signs = jnp.where(live, signs, 0)
    sources = sources.at[0, 0].set(span - 1)
    signs = signs.at[0, 0].set(-1)
    return jnp.stack([sources, pair_ids, signs]).astype(jnp.int32)


def draw_batch_index(key, part):
    groups = NB // BATCH
    scores = jax.random.randint(key, (groups, ROWS_DEV), 0, 1 << 16) * ROWS_DEV + jnp.arange(ROWS_DEV)[None, :]
    scores = scores.at[0, 0].set(-1)
    scores = scores.at[groups - 1, ROWS_DEV - 1].set(-1)
    chosen = jnp.argsort(scores, axis=1)[:, :BATCH] + jnp.arange(groups)[:, None] * ROWS_DEV
    return chosen.reshape(-1).astype(jnp.int32)


def draw_exc_alpha(key, part):
    return make_lists(jax.random.fold_in(key, 11), NB, NA)


def draw_exc_beta(key, part):
    return make_lists(jax.random.fold_in(key, 12), NBETA, NBETA)


def levels(own_key, dims, pieces, low, high):
    def one(axis_at, parts):
        steps = jax.random.uniform(jax.random.fold_in(jax.random.fold_in(own_key, 6), axis_at), (parts,), jnp.float32, low / len(pieces), high / len(pieces))
        return jnp.repeat(jnp.exp(steps), dims[axis_at] // parts).reshape((-1,) + (1,) * (len(dims) - axis_at - 1))

    level = one(*pieces[0])
    for cut in pieces[1:]:
        level = level * one(*cut)
    return level


def centred(rng, extent, deviation, bound, cuts=(), kind=jnp.bfloat16):
    factor_of = levels(rng, extent, cuts, -0.22, 0.18) if cuts else 1.0
    drawn = jax.random.normal(rng, extent, jnp.float32) * deviation * factor_of
    return jnp.minimum(jnp.maximum(drawn, -bound), bound).astype(kind)


def setup_inputs(seed: int = 0) -> dict:
    key_of = jax.random.split(jax.random.key(seed), 6)
    return {
        "civec": centred(key_of[0], (NA, NBETA), 1.0, 6.0, ((0, 4), (1, 64)), jnp.float32),
        "batch_index": draw_batch_index(jax.random.fold_in(key_of[5], 71), 0),
        "exc_alpha": draw_exc_alpha(jax.random.fold_in(key_of[5], 71), 0),
        "exc_beta": draw_exc_beta(jax.random.fold_in(key_of[5], 71), 0),
        "one_body": centred(key_of[4], (PAIRS,), NEXC ** -0.5, 0.625, (), jnp.float32),
    }


def reference(civec, batch_index, exc_alpha, exc_beta, one_body):
    highest = lax.Precision.HIGHEST
    pair_range = jnp.arange(PAIRS, dtype=jnp.int32)
    columns = jnp.arange(NBETA, dtype=jnp.int32)[:, None]
    beta_signs = exc_beta[2].astype(jnp.float32)

    def string_step(totals, string_index):
        batch_row = civec[batch_index[string_index]]
        sources = exc_alpha[0, string_index]
        pair_ids = exc_alpha[1, string_index]
        alpha_signs = exc_alpha[2, string_index].astype(jnp.float32)
        placing = (pair_ids[:, None] == pair_range[None, :]).astype(jnp.float32) * alpha_signs[:, None]
        d_alpha = jnp.dot(placing.T, civec[sources], precision=highest)
        values = batch_row[exc_beta[0]] * beta_signs
        d_beta = jnp.zeros((PAIRS, NBETA), jnp.float32).at[exc_beta[1], columns].add(values)
        sigma_row = jnp.dot(one_body, d_alpha + d_beta, precision=highest)
        one_part = jnp.stack([jnp.dot(d_alpha, batch_row, precision=highest), jnp.dot(d_beta, batch_row, precision=highest)])
        same_part = jnp.dot(d_alpha, d_alpha.T, precision=highest)
        mixed_part = jnp.dot(d_alpha, d_beta.T, precision=highest)
        return ((totals[0] + one_part, totals[1] + same_part, totals[2] + mixed_part), sigma_row)
    start_totals = (jnp.zeros((2, PAIRS), jnp.float32), jnp.zeros((PAIRS, PAIRS), jnp.float32), jnp.zeros((PAIRS, PAIRS), jnp.float32))
    totals, sigma = lax.scan(string_step, start_totals, jnp.arange(NB, dtype=jnp.int32))
    norm_count = NB * NBETA
    root_count = math.sqrt(norm_count)
    return (sigma, totals[0] / root_count, totals[1] / norm_count, totals[2] / root_count)
```

```python
import functools
import math

import jax
import jax.numpy as jnp
from jax import lax
from jax.experimental import pallas as pl
from jax.experimental.pallas import tpu as pltpu
from jax.sharding import PartitionSpec as P

MESH = pl.DeviceIdType.MESH
F32, BF16, I32 = jnp.float32, jnp.bfloat16, jnp.int32
LANES = 128
HALF = 42
SHIFT = 68
ROWS = 168
NT = (((1,), (1,)), ((), ()))
NN = (((1,), (0,)), ((), ()))


def split(x):
    high = x.astype(BF16)
    return high, (x - high.astype(F32)).astype(BF16)


def dot(a, b, dims):
    return lax.dot_general(a, b, dims, preferred_element_type=F32)


def dot3(a, b, dims):
    return dot(a[0], b[0], dims) + (dot(a[0], b[1], dims) + dot(a[1], b[0], dims))


def dot2(a, b, dims):
    return dot(a, b[0], dims) + dot(a, b[1], dims)


def barrel(x, amount, bits, width):
    for bit in range(bits):
        moved = pltpu.roll(x, 1 << bit, 1)
        x = jnp.where(lax.rem(lax.div(amount, 1 << bit), 2) == 1, moved, x)
    return x


def spread_kernel(groups, parts, rows_ref, civ_ref, table_ref, blocks_ref, own_sem, ssem, rsem, xs, xr):
    ga = lax.axis_index("alpha")
    me = lax.axis_index("beta")
    barrier = pltpu.get_barrier_semaphore()

    def greet(d, c):
        pl.semaphore_signal(barrier, inc=1, device_id=(ga, lax.rem(me + d, parts)), device_id_type=MESH)
        return c

    lax.fori_loop(1, parts, greet, 0)
    for d in range(1, groups):
        pl.semaphore_signal(barrier, inc=1, device_id=(lax.rem(ga + d, groups), me), device_id_type=MESH)
    pl.semaphore_wait(barrier, parts - 1 + groups - 1)

    def row_copy(j, slot):
        return pltpu.make_async_remote_copy(
            rows_ref, table_ref.at[slot], ssem.at[j], rsem.at[slot], device_id=(ga, j), device_id_type=MESH
        )

    def send(d, c):
        row_copy(lax.rem(me + d, parts), me).start()
        return c

    lax.fori_loop(1, parts, send, 0)
    own = pltpu.make_async_copy(rows_ref, table_ref.at[me], own_sem)
    own.start()
    blocks = []
    for d in range(1, groups):
        copy = pltpu.make_async_remote_copy(
            civ_ref, blocks_ref.at[groups - 1 - d], xs.at[d - 1], xr.at[groups - 1 - d],
            device_id=(lax.rem(ga + d, groups), me), device_id_type=MESH,
        )
        copy.start()
        blocks.append(copy)
    own.wait()

    def finish(d, c):
        j = lax.rem(me + d, parts)
        copy = row_copy(j, j)
        copy.wait_send()
        copy.wait_recv()
        return c

    lax.fori_loop(1, parts, finish, 0)
    for copy in blocks:
        copy.wait_send()
    for d in range(1, groups):
        blocks[d - 1].wait_recv()


def pick_kernel(parts, slots, batch, src_ref, sign_ref, local_ref, code_ref, table_ref, civ_ref, blocks_ref, rows_ref,
                vals_ref, a_ref):
    ga = lax.axis_index("alpha")
    groups = lax.axis_size("alpha")
    rows_dev = civ_ref.shape[0]
    deep = code_ref.shape[1]
    tiles = deep // 8
    for lt in range(3):
        codes = [code_ref[lt, pl.ds(8 * i, 8), :] for i in range(tiles)]
        low = [jnp.bitwise_and(c, 127) for c in codes]
        high = [jnp.bitwise_and(lax.shift_right_logical(c, 7), 255) for c in codes]

        def step(j, acc):
            acc = list(acc)
            for t in range(3):
                row0 = jnp.broadcast_to(table_ref[j, pl.ds(t, 1), :], (8, LANES))
                row1 = jnp.broadcast_to(table_ref[j, pl.ds(3 + t, 1), :], (8, LANES))
                for i in range(tiles):
                    hit = high[i] == 3 * j + t
                    acc[2 * i] = jnp.where(hit, jnp.take_along_axis(row0, low[i], 1, mode="promise_in_bounds"), acc[2 * i])
                    acc[2 * i + 1] = jnp.where(hit, jnp.take_along_axis(row1, low[i], 1, mode="promise_in_bounds"), acc[2 * i + 1])
            return tuple(acc)

        acc = lax.fori_loop(0, parts, step, (jnp.zeros((8, LANES), F32),) * (2 * tiles))
        for i in range(tiles):
            sign = (lax.shift_right_logical(codes[i], 24) - 1).astype(F32)
            vals_ref[0, lt, pl.ds(8 * i, 8), :] = acc[2 * i] * sign
            vals_ref[1, lt, pl.ds(8 * i, 8), :] = acc[2 * i + 1] * sign

    a_ref[...] = jnp.zeros_like(a_ref)

    def take(k, c):
        for b in range(batch):
            source = src_ref[b * slots + k]
            away = lax.rem(lax.div(source, rows_dev) - ga + groups, groups)
            inner = lax.rem(source, rows_dev)
            mine = civ_ref[pl.ds(inner, 1), :]
            other = blocks_ref[jnp.maximum(away - 1, 0), pl.ds(inner, 1), :]
            sign = sign_ref[b * slots + k].astype(F32)
            a_ref[pl.ds(b * (slots + 1) + k, 1), :] = jnp.where(away == 0, mine, other) * sign
        return c

    lax.fori_loop(0, slots, take, 0)
    for b in range(batch):
        inner = local_ref[b]
        a_ref[pl.ds(b * (slots + 1) + slots, 1), :] = civ_ref[pl.ds(inner, 1), :]


def reduce_kernel(groups, shape, slots, pairs, vals_ref, code_ref, a_ref, own_pair_ref, pair_ref, ext_ref, hrow_ref, hcol_ref,
                  sigma_ref, mixed_ref, same_ref,
                  d_ref, tiles_ref, got_ref, zbuf, gat, all_ref,
                  ssem, rsem, zs, zr, fs, fr, cs, cr):
    nz, ny, nc = shape
    parts = nz * ny * nc
    per = 64 // parts
    ga = lax.axis_index("alpha")
    me = lax.axis_index("beta")
    z, y, core = me // (ny * nc), (me // nc) % ny, me % nc
    planes = groups * ny

    def at(zz, yy, cc):
        return (zz * ny + yy) * nc + cc

    barrier = pltpu.get_barrier_semaphore()

    def greet(d, c):
        pl.semaphore_signal(barrier, inc=1, device_id=(ga, lax.rem(me + d, parts)), device_id_type=MESH)
        return c

    lax.fori_loop(1, parts, greet, 0)
    around = []
    for k in range(1, planes):
        around.append((lax.rem(ga + k // ny, groups), lax.rem(y + k % ny, ny)))
    extra = 0
    for k, (aa, yy) in enumerate(around, 1):
        if k // ny:
            pl.semaphore_signal(barrier, inc=1, device_id=(aa, at(z, yy, core)), device_id_type=MESH)
            extra += 1

    width = a_ref.shape[1]
    deep = d_ref.shape[1]
    step_rows = 112
    for lt in range(width // LANES):
        cut = pl.ds(lt * LANES, LANES)
        for base in range(0, deep, step_rows):
            size = min(step_rows, deep - base)
            ids = lax.broadcasted_iota(I32, (size, LANES), 0) + base

            def place(e, acc):
                hit = jnp.bitwise_and(lax.shift_right_logical(code_ref[lt, pl.ds(e, 1), :], 15), 511) == ids
                return (
                    jnp.where(hit, vals_ref[0, lt, pl.ds(e, 1), :], acc[0]),
                    jnp.where(hit, vals_ref[1, lt, pl.ds(e, 1), :], acc[1]),
                )

            acc = lax.fori_loop(0, slots, place, (jnp.zeros((size, LANES), F32),) * 2)
            d_ref[0, pl.ds(base, size), cut] = acc[0]
            d_ref[1, pl.ds(base, size), cut] = acc[1]

    a = a_ref[...]
    a2 = split(a)
    d2 = [split(d_ref[b]) for b in range(2)]
    string = slots + 1
    row = lax.broadcasted_iota(I32, (ROWS, 1), 0)
    first = row < string
    col_row = lax.broadcasted_iota(I32, (1, ROWS), 1)
    one_hot = (lax.broadcasted_iota(I32, (deep, ROWS), 0) == own_pair_ref[...]).astype(F32)
    weight = jnp.sum(one_hot * hcol_ref[...], axis=0, keepdims=True)
    own_first = jnp.broadcast_to(jnp.where(col_row < string, weight, 0.0), (8, ROWS))
    own_second = jnp.broadcast_to(jnp.where(col_row < string, 0.0, weight), (8, ROWS))
    hrow = split(jnp.broadcast_to(hrow_ref[...], (8, deep)))
    sigma_ref[0:1, :] = (dot3(split(own_first), a2, NN) + dot3(hrow, d2[0], NN))[0:1]
    sigma_ref[1:2, :] = (dot3(split(own_second), a2, NN) + dot3(hrow, d2[1], NN))[0:1]
    m = jnp.where(first, dot3(a2, d2[0], NT), dot3(a2, d2[1], NT))
    ext_i = lax.broadcasted_iota(I32, (LANES, ROWS), 0)
    ext_j = lax.broadcasted_iota(I32, (LANES, ROWS), 1)
    wrapped = jnp.where(ext_i >= string, ext_i - string, ext_i)
    grams = []
    for b in range(2):
        perm = (ext_j == wrapped + b * string).astype(BF16)
        ext = tuple(dot(perm, part, NN).astype(BF16) for part in a2)
        grams.append(dot3(a2, ext, NT))
    gram = jnp.where(first, grams[0], grams[1])
    local = jnp.where(first, row, row - string)
    folded = barrel(gram, lax.rem(SHIFT - local + 2 * LANES, LANES), 7, LANES)
    lane = lax.broadcasted_iota(I32, (ROWS, LANES), 1)
    tail = jnp.concatenate([m[:, 2 * LANES :], jnp.zeros((ROWS, 3 * LANES - deep), F32)], axis=1)
    last = jnp.where(lane < SHIFT, tail, jnp.where(lane < SHIFT + HALF, folded, 0.0))
    for rg in range(ROWS // 8):
        for lt in range(3):
            k = rg * 3 + lt
            piece = last if lt == 2 else m[:, lt * LANES : (lt + 1) * LANES]
            tiles_ref[k // per, k % per] = piece[8 * rg : 8 * rg + 8]
    tiles_ref[parts - 1, per - 1] = jnp.zeros((8, LANES), F32)

    pl.semaphore_wait(barrier, parts - 1 + extra)

    def part_copy(j, slot):
        return pltpu.make_async_remote_copy(
            tiles_ref.at[j], got_ref.at[slot], ssem.at[j], rsem.at[slot], device_id=(ga, j), device_id_type=MESH
        )

    def send(d, c):
        part_copy(lax.rem(me + d, parts), me).start()
        return c

    lax.fori_loop(1, parts, send, 0)
    got_ref[me] = tiles_ref[me]

    def finish(d, c):
        j = lax.rem(me + d, parts)
        part_copy(j, j).wait_recv()
        return c

    lax.fori_loop(1, parts, finish, 0)
    zbuf[z] = jnp.sum(got_ref[...], axis=0)

    def z_copy(zz, slot):
        return pltpu.make_async_remote_copy(
            zbuf.at[slot], zbuf.at[slot], zs.at[zz], zr.at[slot], device_id=(ga, at(zz, y, core)), device_id_type=MESH
        )

    for k in range(1, nz):
        z_copy(lax.rem(z + k, nz), z).start()
    for k in range(1, nz):
        zz = lax.rem(z + k, nz)
        z_copy(zz, zz).wait_recv()

    def plane_copy(src, aa, yy, slot_a, slot_y):
        return pltpu.make_async_remote_copy(
            src, gat.at[slot_a, slot_y, core], fs.at[aa, yy], fr.at[slot_a, slot_y],
            device_id=(aa, at(z, yy, core)), device_id_type=MESH,
        )

    def twin_copy(src, slot_a, slot_y, slot_c):
        return pltpu.make_async_remote_copy(
            src, gat.at[slot_a, slot_y, slot_c], cs.at[slot_a, slot_y], cr.at[slot_a, slot_y],
            device_id=(ga, at(z, y, 1 - core)), device_id_type=MESH,
        )

    for aa, yy in around:
        plane_copy(zbuf, aa, yy, ga, y).start()
    twin_copy(zbuf, ga, y, core).start()
    gat[ga, y, core] = zbuf[...]
    for aa, yy in around:
        plane_copy(zbuf, aa, yy, aa, yy).wait_recv()
        twin_copy(gat.at[aa, yy, core], aa, yy, core).start()
    for aa, yy in [(ga, y)] + around:
        twin_copy(zbuf, aa, yy, 1 - core).wait_recv()

    for a_ in range(groups):
        for rg in range(ROWS // 8):
            for lt in range(3):
                k = rg * 3 + lt
                j, s = k // per, k % per
                all_ref[pl.ds(a_ * ROWS + 8 * rg, 8), pl.ds(lt * LANES, LANES)] = gat[
                    a_, (j // nc) % ny, j % nc, j // (ny * nc), s
                ]
    placing = (lax.broadcasted_iota(I32, (deep, groups * ROWS), 0) == pair_ref[...]).astype(BF16)
    mixed_ref[...] = dot2(placing, split(all_ref[...]), NN)
    weights = jnp.where((lane == SHIFT) | (lane == SHIFT + HALF - 1), 0.5, 1.0)
    weights = jnp.where((lane >= SHIFT) & (lane < SHIFT + HALF), weights, 0.0)
    amount = lax.rem(local - SHIFT + 2 * LANES, LANES)
    for a_ in range(groups):
        half = all_ref[pl.ds(a_ * ROWS, ROWS), pl.ds(2 * LANES, LANES)] * weights
        half = barrel(half, amount, 7, LANES)
        both = jnp.concatenate([jnp.where(first, half, 0.0), jnp.where(first, 0.0, half)], axis=1)
        right = (lax.broadcasted_iota(I32, (3 * LANES, 2 * LANES), 0) == ext_ref[pl.ds(a_, 1), :]).astype(BF16)
        all_ref[pl.ds(a_ * ROWS, ROWS), :] = sum(dot(p, right, NT) for p in split(both))
    upper = dot2(placing, split(all_ref[...]), NN)
    square = jnp.concatenate([upper, jnp.zeros((3 * LANES - deep, 3 * LANES), F32)], axis=0)
    same_ref[...] = (square + square.T)[:deep]

    def drain(d, c):
        j = lax.rem(me + d, parts)
        part_copy(j, j).wait_send()
        return c

    lax.fori_loop(1, parts, drain, 0)
    for k in range(1, nz):
        z_copy(lax.rem(z + k, nz), z).wait_send()
    for aa, yy in around:
        plane_copy(zbuf, aa, yy, ga, y).wait_send()
    for aa, yy in [(ga, y)] + around:
        twin_copy(zbuf, aa, yy, core).wait_send()


def body(shape, civec, batch_index, exc_alpha, exc_beta, one_body):
    vmem = pl.BlockSpec(memory_space=pltpu.VMEM)
    smem = pl.BlockSpec(memory_space=pltpu.SMEM)
    anywhere = pl.BlockSpec(memory_space=pl.ANY)
    nz, ny, nc = shape
    parts = nz * ny * nc
    per = 64 // parts
    ga = lax.axis_index("alpha")
    groups = lax.axis_size("alpha")
    rows_dev, width = civec.shape
    total = batch_index.shape[0]
    batch = total // groups
    slots = exc_alpha.shape[2]
    pairs = one_body.shape[0]
    deep = -(-pairs // 8) * 8
    slots_deep = -(-slots // 8) * 8
    local = lax.dynamic_slice_in_dim(batch_index, ga * batch, batch) - ga * rows_dev
    mine = lax.dynamic_slice_in_dim(exc_alpha, ga * batch, batch, 1)
    batch_rows = jnp.concatenate([lax.dynamic_slice_in_dim(civec, local[b], 1, 0) for b in range(batch)], 0)
    code = exc_beta[0] + exc_beta[1] * 32768 + (exc_beta[2] + 1) * (1 << 24)
    code = jnp.pad(code.T, ((0, slots_deep - slots), (0, 0)), constant_values=(511 << 15) + (1 << 24))
    code = code.reshape(slots_deep, 3, LANES).swapaxes(0, 1)
    pair_all = jnp.pad(exc_alpha[1], ((0, 0), (0, 1)), constant_values=pairs)
    pair_rows = jnp.pad(pair_all.reshape(groups, batch * (slots + 1)), ((0, 0), (0, ROWS - batch * (slots + 1))), constant_values=511)
    own_pair = lax.dynamic_slice_in_dim(pair_rows, ga, 1, 0)
    ext = jnp.concatenate([pair_all, pair_all[:, : LANES - slots - 1]], axis=1).reshape(groups, batch * LANES)
    hpad = jnp.pad(one_body, (0, deep - pairs))

    table, blocks = pl.pallas_call(
        functools.partial(spread_kernel, groups, parts),
        out_shape=(
            jax.ShapeDtypeStruct((parts, 6, LANES), F32),
            jax.ShapeDtypeStruct((groups - 1, rows_dev, width), F32),
        ),
        in_specs=[vmem, anywhere],
        out_specs=(anywhere, anywhere),
        scratch_shapes=[
            pltpu.SemaphoreType.DMA,
            pltpu.SemaphoreType.DMA((parts,)),
            pltpu.SemaphoreType.DMA((parts,)),
            pltpu.SemaphoreType.DMA((groups - 1,)),
            pltpu.SemaphoreType.DMA((groups - 1,)),
        ],
        compiler_params=pltpu.CompilerParams(collective_id=0, has_side_effects=True),
        name="spread",
    )(batch_rows.reshape(batch * 3, LANES), civec)

    vals, arows = pl.pallas_call(
        functools.partial(pick_kernel, parts, slots, batch),
        out_shape=(
            jax.ShapeDtypeStruct((batch, 3, slots_deep, LANES), F32),
            jax.ShapeDtypeStruct((ROWS, width), F32),
        ),
        in_specs=[smem, smem, smem, vmem, vmem, vmem, vmem, vmem],
        out_specs=(vmem, vmem),
        name="pick",
    )(mine[0].reshape(-1), mine[2].reshape(-1), local, code, table, civec, blocks, batch_rows)

    sigma, mixed, same = pl.pallas_call(
        functools.partial(reduce_kernel, groups, shape, slots, pairs),
        out_shape=(
            jax.ShapeDtypeStruct((batch, width), F32),
            jax.ShapeDtypeStruct((deep, 3 * LANES), F32),
            jax.ShapeDtypeStruct((deep, 3 * LANES), F32),
        ),
        in_specs=[vmem] * 8,
        out_specs=(vmem, vmem, vmem),
        scratch_shapes=[
            pltpu.VMEM((2, deep, width), F32),
            pltpu.VMEM((parts, per, 8, LANES), F32),
            pltpu.VMEM((parts, per, 8, LANES), F32),
            pltpu.VMEM((nz, per, 8, LANES), F32),
            pltpu.VMEM((groups, ny, nc, nz, per, 8, LANES), F32),
            pltpu.VMEM((groups * ROWS, 3 * LANES), F32),
            pltpu.SemaphoreType.DMA((parts,)),
            pltpu.SemaphoreType.DMA((parts,)),
            pltpu.SemaphoreType.DMA((nz,)),
            pltpu.SemaphoreType.DMA((nz,)),
            pltpu.SemaphoreType.DMA((groups, ny)),
            pltpu.SemaphoreType.DMA((groups, ny)),
            pltpu.SemaphoreType.DMA((groups, ny)),
            pltpu.SemaphoreType.DMA((groups, ny)),
        ],
        compiler_params=pltpu.CompilerParams(collective_id=1, has_side_effects=True),
        name="reduce",
    )(vals, code, arows, own_pair, pair_rows.reshape(1, groups * ROWS), ext, hpad[None], hpad[:, None])

    norm = total * width * parts
    root = math.sqrt(norm)
    density = jnp.stack([same[:pairs, pairs], mixed[pairs, :pairs]]) / root
    return sigma, density, same[:pairs, :pairs] / norm, mixed[:pairs, :pairs] / root


def solution(mesh, shape=(8, 4, 2)):
    in_specs = (P("alpha", "beta"), P(), P(), P(None, "beta", None), P())
    out_specs = (P("alpha", "beta"), P(), P(), P())
    return jax.shard_map(
        functools.partial(body, shape), mesh=mesh, in_specs=in_specs, out_specs=out_specs, check_vma=False
    )
```

```python
import functools
import math

import jax
import jax.numpy as jnp
from jax import lax
from jax.experimental import pallas as pl
from jax.experimental.pallas import tpu as pltpu
from jax.sharding import PartitionSpec as P

MESH = pl.DeviceIdType.MESH
F32, BF16, I32 = jnp.float32, jnp.bfloat16, jnp.int32
LANES = 128
HALF = 42
SHIFT = 68
ROWS = 168
EMPTY = 511
NT = (((1,), (1,)), ((), ()))
NN = (((1,), (0,)), ((), ()))
ALONG = lax.GatherDimensionNumbers(
    offset_dims=(), collapsed_slice_dims=(1,), start_index_map=(1,), operand_batching_dims=(0,), start_indices_batching_dims=(0,)
)


def split(x):
    high = x.astype(BF16)
    return high, (x - high.astype(F32)).astype(BF16)


def dot(a, b, dims):
    return lax.dot_general(a, b, dims, preferred_element_type=F32)


def dot3(a, b, dims):
    return dot(a[0], b[0], dims) + (dot(a[0], b[1], dims) + dot(a[1], b[0], dims))


def dot2(a, b, dims):
    return dot(a, b[0], dims) + dot(a, b[1], dims)


def lanes_of(x, index):
    return lax.gather(x, index[..., None], ALONG, (1, 1), mode=lax.GatherScatterMode.PROMISE_IN_BOUNDS)


def barrel(x, amount, bits):
    for bit in range(bits):
        moved = pltpu.roll(x, 1 << bit, 1)
        x = jnp.where(lax.rem(lax.div(amount, 1 << bit), 2) == 1, moved, x)
    return x


def packed_row(wide_ref, first, second, slots, end_first, end_second):
    string = slots + 1
    wide_ref[...] = jnp.zeros_like(wide_ref)
    wide_ref[0:1, 0:slots] = first
    wide_ref[1:2, 0:slots] = second
    lane = lax.broadcasted_iota(I32, (1, 2 * LANES), 1)
    blank = jnp.zeros((1, LANES), F32)
    one = jnp.concatenate([wide_ref[0:1, :], blank], axis=1)
    two = pltpu.roll(jnp.concatenate([wide_ref[1:2, :], blank], axis=1), string, 1)
    out = jnp.where(lane < string, one, two)
    out = jnp.where(lane == slots, end_first, jnp.where(lane == string + slots, end_second, out))
    return jnp.where(lane < 2 * string, out, float(EMPTY))


def main_kernel(groups, shape, slots, pairs, batch_ref, exc_ref, beta_ref, h_ref, civ_ref, sigma_ref, gat,
                code_n, code_ref, inv_ref, rows_s, table, texp, vals_ref, blk_ref, a_ref, wide_ref,
                tiles_ref, got_ref, zbuf,
                ts, tr, xs, xr, ssem, rsem, zs, zr, fs, fr, cs, cr):
    nz, ny, nc = shape
    parts = nz * ny * nc
    per = 64 // parts
    width = beta_ref.shape[1]
    cuts = width // LANES
    deep = 3 * LANES
    slots_deep = code_ref.shape[1]
    rows_dev = civ_ref.shape[0]
    string = slots + 1
    ga = lax.axis_index("alpha")
    me = lax.axis_index("beta")
    z, y, core = me // (ny * nc), (me // nc) % ny, me % nc
    planes = groups * ny

    def at(zz, yy, cc):
        return (zz * ny + yy) * nc + cc

    barrier = pltpu.get_barrier_semaphore()

    def greet(d, c):
        pl.semaphore_signal(barrier, inc=1, device_id=(ga, lax.rem(me + d, parts)), device_id_type=MESH)
        return c

    around = [(lax.rem(ga + k // ny, groups), lax.rem(y + k % ny, ny), k // ny) for k in range(1, planes)]
    extra = 0
    for aa, yy, off in around:
        if off:
            pl.semaphore_signal(barrier, inc=1, device_id=(aa, at(z, yy, core)), device_id_type=MESH)
            extra += 1
    lax.fori_loop(1, parts, greet, 0)

    for b in range(2):
        row = civ_ref[pl.ds(lax.rem(batch_ref[2 * ga + b], rows_dev), 1), :]
        for t in range(cuts):
            rows_s[b * cuts + t : b * cuts + t + 1, :] = row[:, t * LANES : (t + 1) * LANES]

    code_n[...] = jnp.full(code_n.shape, (EMPTY << 15) + (1 << 24), I32)
    code_n[:, 0:slots] = beta_ref[0] + beta_ref[1] * 32768 + (beta_ref[2] + 1) * (1 << 24)
    for lt in range(cuts):
        code_ref[lt] = code_n[lt * LANES : (lt + 1) * LANES, :].T[0:slots_deep]

    def invert(lt):
        for base in range(0, deep, LANES):
            ids = lax.broadcasted_iota(I32, (LANES, LANES), 0) + base

            def mark(e, acc):
                pair = jnp.bitwise_and(lax.shift_right_logical(code_ref[lt, pl.ds(e, 1), :], 15), 511)
                return jnp.where(pair == ids, e, acc)

            if base < pairs:
                acc = lax.fori_loop(0, slots, mark, jnp.full((LANES, LANES), LANES - 1, I32))
                inv_ref[lt * LANES : (lt + 1) * LANES, base : base + LANES] = acc.T

    for lt in range(cuts):
        invert(lt)

    pl.semaphore_wait(barrier, parts - 1 + extra)

    def row_copy(j, slot):
        return pltpu.make_async_remote_copy(
            rows_s, table.at[slot], ts.at[j], tr.at[slot], device_id=(ga, j), device_id_type=MESH
        )

    def send_row(d, c):
        row_copy(lax.rem(me + d, parts), me).start()
        return c

    lax.fori_loop(1, parts, send_row, 0)

    right, left = lax.rem(ga + 1, groups), lax.rem(ga + groups - 1, groups)
    half_rows = rows_dev // 2

    def block_copy(src, dst, k, to):
        return pltpu.make_async_remote_copy(
            src, dst, xs.at[k], xr.at[k], device_id=(to, me), device_id_type=MESH
        )

    first_half, second_half = pl.ds(0, half_rows), pl.ds(half_rows, half_rows)
    hops = [
        block_copy(civ_ref, blk_ref.at[0], 0, right),
        block_copy(civ_ref, blk_ref.at[1], 1, left),
        block_copy(blk_ref.at[0, first_half], blk_ref.at[2, first_half], 2, right),
        block_copy(blk_ref.at[1, second_half], blk_ref.at[2, second_half], 3, left),
    ]
    if groups == 2:
        hops = hops[:1]
    for hop in hops[:2]:
        hop.start()
    table[me] = rows_s[...]

    s_row = packed_row(
        wide_ref, exc_ref[0, pl.ds(2 * ga, 1), :].astype(F32), exc_ref[0, pl.ds(2 * ga + 1, 1), :].astype(F32), slots,
        batch_ref[2 * ga].astype(F32), batch_ref[2 * ga + 1].astype(F32),
    )
    g_row = packed_row(
        wide_ref, exc_ref[2, pl.ds(2 * ga, 1), :].astype(F32), exc_ref[2, pl.ds(2 * ga + 1, 1), :].astype(F32), slots, 1.0, 1.0
    )
    p_row = packed_row(
        wide_ref, exc_ref[1, pl.ds(2 * ga, 1), :].astype(F32), exc_ref[1, pl.ds(2 * ga + 1, 1), :].astype(F32), slots,
        float(pairs), float(pairs),
    )
    lane = lax.broadcasted_iota(I32, (1, 2 * LANES), 1)
    g_row = jnp.where(lane < 2 * string, g_row, 0.0)
    meta = jnp.concatenate([s_row, g_row, jnp.zeros((6, 2 * LANES), F32)], axis=0).T[0:ROWS]
    source, sign = meta[:, 0:1], meta[:, 1:2]

    def choose(block, owner):
        ids = (lax.broadcasted_iota(I32, (ROWS, rows_dev), 1) + owner * rows_dev).astype(F32)
        pick = jnp.where(source == ids, sign, 0.0).astype(BF16)
        parts2 = split(block)
        return dot(pick, parts2[0], NN), dot(pick, parts2[1], NN)

    a_high, a_low = choose(civ_ref[...], ga)

    def finish_row(d, c):
        j = lax.rem(me + d, parts)
        row_copy(j, j).wait_recv()
        return c

    lax.fori_loop(1, parts, finish_row, 0)

    def widen(j, c):
        for b in range(2):
            for t in range(cuts):
                texp[b, cuts * j + t] = jnp.broadcast_to(table[j, b * cuts + t : b * cuts + t + 1, :], (8, LANES))
        return c

    lax.fori_loop(0, parts, widen, 0)

    total_rows = parts * cuts
    chunk = 24 if total_rows % 24 == 0 else total_rows
    steps = chunk // 8 if chunk % 8 == 0 else 0

    def look_up(i, c):
        start = pl.multiple_of(8 * i, 8)
        for lt in range(cuts):
            code = code_ref[lt, pl.ds(start, 8), :]
            low = jnp.bitwise_and(code, 127)
            high = jnp.bitwise_and(lax.shift_right_logical(code, 7), 255)
            group = lax.shift_right_logical(high, 3)
            acc = [jnp.zeros((8, LANES), F32)] * 2
            index = jnp.broadcast_to(low[None], (chunk, 8, LANES)).reshape(chunk * 8, LANES)
            for base in range(0, total_rows, chunk):
                for b in range(2):
                    got = texp[b, base : base + chunk].reshape(chunk * 8, LANES)
                    got = lanes_of(got, index).reshape(chunk, 8, LANES)
                    for bit in range(3):
                        n = got.shape[0] // 2
                        got = got.reshape(n, 2, 8, LANES)
                        mask = jnp.broadcast_to(jnp.bitwise_and(high, 1 << bit)[None], (n, 8, LANES)) != 0
                        got = jnp.where(mask, got[:, 1], got[:, 0])
                    for k in range(steps):
                        acc[b] = jnp.where(group == base // 8 + k, got[k], acc[b])
            factor = (lax.shift_right_logical(code, 24) - 1).astype(F32)
            vals_ref[0, lt, pl.ds(start, 8), :] = acc[0] * factor
            vals_ref[1, lt, pl.ds(start, 8), :] = acc[1] * factor
        return c

    tiles = slots_deep // 8
    relay = tiles // 2
    lax.fori_loop(0, relay, look_up, 0)
    for hop in hops[:2]:
        hop.wait_recv()
    for hop in hops[2:]:
        hop.start()
    lax.fori_loop(relay, tiles, look_up, 0)

    blank = jnp.zeros((LANES - slots_deep, LANES), F32)
    d2 = []
    for b in range(2):
        by_slot = jnp.concatenate(
            [jnp.concatenate([vals_ref[b, lt], blank], axis=0).T for lt in range(cuts)], axis=0
        )
        d2.append(split(jnp.concatenate(
            [lanes_of(by_slot, inv_ref[:, base : base + LANES]) for base in range(0, deep, LANES)], axis=1
        )))

    for hop in hops[2:]:
        hop.wait_recv()
    owners = [lax.rem(ga + groups - 1, groups), lax.rem(ga + 1, groups), lax.rem(ga + 2, groups)]
    for k in range(groups - 1):
        more = choose(blk_ref[k], owners[k])
        a_high, a_low = a_high + more[0], a_low + more[1]
    a2 = (a_high.astype(BF16), a_low.astype(BF16))

    row = lax.broadcasted_iota(I32, (ROWS, 1), 0)
    first = row < string
    col_row = lax.broadcasted_iota(I32, (1, ROWS), 1)
    own = (lax.broadcasted_iota(I32, (deep, ROWS), 0).astype(F32) == p_row[:, 0:ROWS]).astype(BF16)
    wide_ref[...] = jnp.zeros_like(wide_ref)
    a_ref[...] = jnp.zeros_like(a_ref)
    a_ref[0:1, 0:pairs] = h_ref[...].reshape(1, pairs)
    hrow = split(jnp.broadcast_to(a_ref[0:1, :], (8, deep)))
    weight = dot(hrow[0], own, NN) + dot(hrow[1], own, NN)
    for b in range(2):
        part = jnp.where((col_row < string) == (b == 0), weight, 0.0)
        sigma_ref[b : b + 1, :] = (dot3(split(part), a2, NN) + dot3(hrow, d2[b], NT))[0:1]
    m = jnp.where(first, dot3(a2, d2[0], NN), dot3(a2, d2[1], NN))
    ext_i = lax.broadcasted_iota(I32, (LANES, ROWS), 0)
    ext_j = lax.broadcasted_iota(I32, (LANES, ROWS), 1)
    wrapped = jnp.where(ext_i >= string, ext_i - string, ext_i)
    grams = []
    for b in range(2):
        perm = (ext_j == wrapped + b * string).astype(BF16)
        ext = tuple(dot(perm, part, NN).astype(BF16) for part in a2)
        grams.append(dot3(a2, ext, NT))
    gram = jnp.where(first, grams[0], grams[1])
    local = jnp.where(first, row, row - string)
    folded = barrel(gram, lax.rem(SHIFT - local + 2 * LANES, LANES), 7)
    lane = lax.broadcasted_iota(I32, (ROWS, LANES), 1)
    last = jnp.where(lane < SHIFT, m[:, 2 * LANES :], jnp.where(lane < SHIFT + HALF, folded, 0.0))
    for rg in range(ROWS // 8):
        for lt in range(3):
            k = rg * 3 + lt
            piece = last if lt == 2 else m[:, lt * LANES : (lt + 1) * LANES]
            tiles_ref[k // per, k % per] = piece[8 * rg : 8 * rg + 8]
    tiles_ref[parts - 1, per - 1] = jnp.zeros((8, LANES), F32)

    def part_copy(j, slot):
        return pltpu.make_async_remote_copy(
            tiles_ref.at[j], got_ref.at[slot], ssem.at[j], rsem.at[slot], device_id=(ga, j), device_id_type=MESH
        )

    def send(d, c):
        part_copy(lax.rem(me + d, parts), me).start()
        return c

    lax.fori_loop(1, parts, send, 0)
    got_ref[me] = tiles_ref[me]

    def finish(d, c):
        j = lax.rem(me + d, parts)
        part_copy(j, j).wait_recv()
        return c

    lax.fori_loop(1, parts, finish, 0)
    zbuf[z] = jnp.sum(got_ref[...], axis=0)

    def z_copy(zz, slot):
        return pltpu.make_async_remote_copy(
            zbuf.at[slot], zbuf.at[slot], zs.at[zz], zr.at[slot], device_id=(ga, at(zz, y, core)), device_id_type=MESH
        )

    for k in range(1, nz):
        z_copy(lax.rem(z + k, nz), z).start()
    for k in range(1, nz):
        zz = lax.rem(z + k, nz)
        z_copy(zz, zz).wait_recv()

    def plane_copy(src, aa, yy, slot_a, slot_y):
        return pltpu.make_async_remote_copy(
            src, gat.at[slot_a, slot_y, core], fs.at[aa, yy], fr.at[slot_a, slot_y],
            device_id=(aa, at(z, yy, core)), device_id_type=MESH,
        )

    def twin_copy(src, slot_a, slot_y, slot_c):
        return pltpu.make_async_remote_copy(
            src, gat.at[slot_a, slot_y, slot_c], cs.at[slot_a, slot_y], cr.at[slot_a, slot_y],
            device_id=(ga, at(z, y, 1 - core)), device_id_type=MESH,
        )

    for aa, yy, _ in around:
        plane_copy(zbuf, aa, yy, ga, y).start()
    twin_copy(zbuf, ga, y, core).start()
    gat[ga, y, core] = zbuf[...]
    for aa, yy, _ in around:
        plane_copy(zbuf, aa, yy, aa, yy).wait_recv()
        twin_copy(gat.at[aa, yy, core], aa, yy, core).start()
    for aa, yy, _ in [(ga, y, 0)] + around:
        twin_copy(zbuf, aa, yy, 1 - core).wait_recv()

    def drain(d, c):
        j = lax.rem(me + d, parts)
        part_copy(j, j).wait_send()
        row_copy(j, j).wait_send()
        return c

    lax.fori_loop(1, parts, drain, 0)
    for hop in hops:
        hop.wait_send()
    for k in range(1, nz):
        z_copy(lax.rem(z + k, nz), z).wait_send()
    for aa, yy, _ in around:
        plane_copy(zbuf, aa, yy, ga, y).wait_send()
    for aa, yy, _ in [(ga, y, 0)] + around:
        twin_copy(zbuf, aa, yy, core).wait_send()


def place_kernel(groups, shape, slots, pairs, norm, exc_ref, gat, sigma_in, sigma_ref, density_ref, same_ref, mixed_ref,
                 r_ref, wide_ref):
    nz, ny, nc = shape
    per = 64 // (nz * ny * nc)
    string = slots + 1
    deep = 3 * LANES
    sigma_ref[...] = sigma_in[...]
    row = lax.broadcasted_iota(I32, (ROWS, 1), 0)
    first = row < string
    local = jnp.where(first, row, row - string)
    amount = lax.rem(local - SHIFT + 2 * LANES, LANES)
    lane = lax.broadcasted_iota(I32, (ROWS, LANES), 1)
    weights = jnp.where((lane == SHIFT) | (lane == SHIFT + HALF - 1), 0.5, 1.0)
    weights = jnp.where((lane >= SHIFT) & (lane < SHIFT + HALF), weights, 0.0)
    strip = lax.broadcasted_iota(I32, (1, LANES), 1)
    mixed = jnp.zeros((deep, deep), F32)
    upper = jnp.zeros((deep, deep), F32)
    for g in range(groups):
        for rg in range(ROWS // 8):
            for lt in range(3):
                k = rg * 3 + lt
                j, s = k // per, k % per
                r_ref[8 * rg : 8 * rg + 8, lt * LANES : (lt + 1) * LANES] = gat[
                    g, (j // nc) % ny, j % nc, j // (ny * nc), s
                ]
        ids = exc_ref[1, 2 * g : 2 * g + 2, :].astype(F32)
        p_row = packed_row(wide_ref, ids[0:1], ids[1:2], slots, float(pairs), float(pairs))
        placing = (lax.broadcasted_iota(I32, (deep, ROWS), 0).astype(F32) == p_row[:, 0:ROWS]).astype(BF16)
        mixed = mixed + dot2(placing, split(r_ref[...]), NN)
        half = barrel(r_ref[:, 2 * LANES :] * weights, amount, 7)
        both = jnp.concatenate([jnp.where(first, half, 0.0), jnp.where(first, 0.0, half)], axis=1)
        ends = []
        for b in range(2):
            line = wide_ref[b : b + 1, :]
            again = pltpu.roll(line, string, 1)
            line = jnp.where(strip < slots, line, jnp.where(strip == slots, float(pairs), again))
            ends.append(line)
        ext = jnp.concatenate(ends, axis=1)
        right = (lax.broadcasted_iota(I32, (deep, 2 * LANES), 0).astype(F32) == ext).astype(BF16)
        t = sum(dot(p, right, NT) for p in split(both))
        upper = upper + dot2(placing, split(t), NN)
    root = math.sqrt(norm)
    same = upper + upper.T
    density_ref[0:1, :] = same[pairs : pairs + 1, 0:pairs] * (1.0 / root)
    density_ref[1:2, :] = mixed[pairs : pairs + 1, 0:pairs] * (1.0 / root)
    same_ref[...] = same[0:pairs, 0:pairs] * (1.0 / norm)
    mixed_ref[...] = mixed[0:pairs, 0:pairs] * (1.0 / root)


def body(shape, civec, batch_index, exc_alpha, exc_beta, one_body):
    vmem = pl.BlockSpec(memory_space=pltpu.VMEM)
    smem = pl.BlockSpec(memory_space=pltpu.SMEM)
    nz, ny, nc = shape
    parts = nz * ny * nc
    per = 64 // parts
    groups = lax.axis_size("alpha")
    rows_dev, width = civec.shape
    total = batch_index.shape[0]
    batch = total // groups
    slots = exc_alpha.shape[2]
    pairs = one_body.shape[0]
    deep = 3 * LANES
    cuts = width // LANES
    slots_deep = -(-slots // 8) * 8
    dma = pltpu.SemaphoreType.DMA
    sigma, gat = pl.pallas_call(
        functools.partial(main_kernel, groups, shape, slots, pairs),
        out_shape=(
            jax.ShapeDtypeStruct((batch, width), F32),
            jax.ShapeDtypeStruct((groups, ny, nc, nz, per, 8, LANES), F32),
        ),
        in_specs=[smem, vmem, vmem, vmem, vmem],
        out_specs=(vmem, vmem),
        scratch_shapes=[
            pltpu.VMEM((width, LANES), I32),
            pltpu.VMEM((cuts, slots_deep, LANES), I32),
            pltpu.VMEM((width, deep), I32),
            pltpu.VMEM((2 * cuts, LANES), F32),
            pltpu.VMEM((parts, 2 * cuts, LANES), F32),
            pltpu.VMEM((2, parts * cuts, 8, LANES), F32),
            pltpu.VMEM((2, cuts, slots_deep, LANES), F32),
            pltpu.VMEM((max(groups - 1, 2), rows_dev, width), F32),
            pltpu.VMEM((8, deep), F32),
            pltpu.VMEM((8, LANES), F32),
            pltpu.VMEM((parts, per, 8, LANES), F32),
            pltpu.VMEM((parts, per, 8, LANES), F32),
            pltpu.VMEM((nz, per, 8, LANES), F32),
            dma((parts,)), dma((parts,)),
            dma((4,)), dma((4,)),
            dma((parts,)), dma((parts,)),
            dma((nz,)), dma((nz,)),
            dma((groups, ny)), dma((groups, ny)),
            dma((groups, ny)), dma((groups, ny)),
        ],
        compiler_params=pltpu.CompilerParams(collective_id=0, has_side_effects=True),
        name="main",
    )(batch_index, exc_alpha, exc_beta, one_body, civec)
    return tuple(pl.pallas_call(
        functools.partial(place_kernel, groups, shape, slots, pairs, total * width * parts),
        out_shape=(
            jax.ShapeDtypeStruct((batch, width), F32),
            jax.ShapeDtypeStruct((2, pairs), F32),
            jax.ShapeDtypeStruct((pairs, pairs), F32),
            jax.ShapeDtypeStruct((pairs, pairs), F32),
        ),
        in_specs=[vmem, vmem, vmem],
        out_specs=(vmem, vmem, vmem, vmem),
        scratch_shapes=[pltpu.VMEM((ROWS, deep), F32), pltpu.VMEM((8, LANES), F32)],
        name="place",
    )(exc_alpha, gat, sigma))


def solution(mesh, shape=(8, 4, 2)):
    in_specs = (P("alpha", "beta"), P(), P(), P(None, "beta", None), P())
    out_specs = (P("alpha", "beta"), P(), P(), P())
    return jax.shard_map(
        functools.partial(body, shape), mesh=mesh, in_specs=in_specs, out_specs=out_specs, check_vma=False
    )
```

```python
import functools
import math

import jax
import jax.numpy as jnp
from jax import lax
from jax.experimental import pallas as pl
from jax.experimental.pallas import tpu as pltpu
from jax.sharding import PartitionSpec as P

MESH = pl.DeviceIdType.MESH
F32, BF16, I32 = jnp.float32, jnp.bfloat16, jnp.int32
LANES = 128
HALF = 42
SHIFT = 68
ROWS = 168
EMPTY = 511
NT = (((1,), (1,)), ((), ()))
NN = (((1,), (0,)), ((), ()))
ALONG = lax.GatherDimensionNumbers(
    offset_dims=(), collapsed_slice_dims=(1,), start_index_map=(1,), operand_batching_dims=(0,), start_indices_batching_dims=(0,)
)


def split(x):
    high = x.astype(BF16)
    return high, (x - high.astype(F32)).astype(BF16)


def dot(a, b, dims):
    return lax.dot_general(a, b, dims, preferred_element_type=F32)


def dot3(a, b, dims):
    return dot(a[0], b[0], dims) + (dot(a[0], b[1], dims) + dot(a[1], b[0], dims))


def dot2(a, b, dims):
    return dot(a, b[0], dims) + dot(a, b[1], dims)


def lanes_of(x, index):
    return lax.gather(x, index[..., None], ALONG, (1, 1), mode=lax.GatherScatterMode.PROMISE_IN_BOUNDS)


def barrel(x, amount, bits):
    for bit in range(bits):
        moved = pltpu.roll(x, 1 << bit, 1)
        x = jnp.where(lax.rem(lax.div(amount, 1 << bit), 2) == 1, moved, x)
    return x


def packed_row(wide_ref, first, second, slots, end_first, end_second):
    string = slots + 1
    wide_ref[...] = jnp.zeros_like(wide_ref)
    wide_ref[0:1, 0:slots] = first
    wide_ref[1:2, 0:slots] = second
    lane = lax.broadcasted_iota(I32, (1, 2 * LANES), 1)
    blank = jnp.zeros((1, LANES), F32)
    one = jnp.concatenate([wide_ref[0:1, :], blank], axis=1)
    two = pltpu.roll(jnp.concatenate([wide_ref[1:2, :], blank], axis=1), string, 1)
    out = jnp.where(lane < string, one, two)
    out = jnp.where(lane == slots, end_first, jnp.where(lane == string + slots, end_second, out))
    return jnp.where(lane < 2 * string, out, float(EMPTY))


def main_kernel(groups, shape, slots, pairs, batch_ref, exc_ref, beta_ref, h_ref, civ_ref, sigma_ref, gat,
                pair_ref, look_ref, sign_ref, hx_ref, inv_ref, rows_s, table, texp, t_ref, vals_ref, blk_ref, line_ref,
                wide_ref, tiles_ref, got_ref, zbuf,
                ts, tr, xs, xr, ssem, rsem, zs, zr, fs, fr, cs, cr):
    nz, ny, nc = shape
    parts = nz * ny * nc
    per = 64 // parts
    width = beta_ref.shape[2]
    cuts = width // LANES
    deep = 3 * LANES
    slots_deep = look_ref.shape[1]
    rows_dev = civ_ref.shape[0]
    string = slots + 1
    ga = lax.axis_index("alpha")
    me = lax.axis_index("beta")
    z, y, core = me // (ny * nc), (me // nc) % ny, me % nc
    planes = groups * ny

    def at(zz, yy, cc):
        return (zz * ny + yy) * nc + cc

    barrier = pltpu.get_barrier_semaphore()

    def greet(d, c):
        pl.semaphore_signal(barrier, inc=1, device_id=(ga, lax.rem(me + d, parts)), device_id_type=MESH)
        return c

    around = [(lax.rem(ga + k // ny, groups), lax.rem(y + k % ny, ny), k // ny) for k in range(1, planes)]
    extra = 0
    for aa, yy, off in around:
        if off:
            pl.semaphore_signal(barrier, inc=1, device_id=(aa, at(z, yy, core)), device_id_type=MESH)
            extra += 1
    lax.fori_loop(1, parts, greet, 0)

    for b in range(2):
        row = civ_ref[pl.ds(lax.rem(batch_ref[2 * ga + b], rows_dev), 1), :]
        for t in range(cuts):
            rows_s[b * cuts + t : b * cuts + t + 1, :] = row[:, t * LANES : (t + 1) * LANES]

    last_tile = slots_deep - 8
    for lt in range(cuts):
        cut = slice(lt * LANES, (lt + 1) * LANES)
        pair_ref[lt, last_tile:, :] = jnp.full((8, LANES), EMPTY, I32)
        look_ref[lt, last_tile:, :] = jnp.zeros((8, LANES), I32)
        sign_ref[lt, last_tile:, :] = jnp.zeros((8, LANES), F32)
        look_ref[lt, 0:slots, :] = beta_ref[0, :, cut]
        pair_ref[lt, 0:slots, :] = beta_ref[1, :, cut]
        sign_ref[lt, 0:slots, :] = beta_ref[2, :, cut].astype(F32)

    blocks = [(lt, base) for base in range(0, pairs, LANES) for lt in range(cuts)]

    def invert(lt, base):
        size = min(LANES, -(-(pairs - base) // 8) * 8)
        ids = lax.broadcasted_iota(I32, (size, LANES), 0) + base

        def mark(e, acc):
            for k in range(9):
                acc = jnp.where(pair_ref[lt, pl.ds(9 * e + k, 1), :] == ids, 9 * e + k, acc)
            return acc

        acc = lax.fori_loop(0, slots // 9, mark, jnp.full((size, LANES), LANES - 1, I32))
        if size < LANES:
            acc = jnp.concatenate([acc, jnp.full((LANES - size, LANES), LANES - 1, I32)], axis=0)
        inv_ref[lt * LANES : (lt + 1) * LANES, base : base + LANES] = acc.T

    early = len(blocks) // 2
    for block in blocks[:early]:
        invert(*block)

    pl.semaphore_wait(barrier, parts - 1 + extra)

    def row_copy(j, slot):
        return pltpu.make_async_remote_copy(
            rows_s, table.at[slot], ts.at[j], tr.at[slot], device_id=(ga, j), device_id_type=MESH
        )

    def send_row(d, c):
        row_copy(lax.rem(me + d, parts), me).start()
        return c

    lax.fori_loop(1, parts, send_row, 0)

    right, left = lax.rem(ga + 1, groups), lax.rem(ga + groups - 1, groups)
    half_rows = rows_dev // 2

    def block_copy(src, dst, k, to):
        return pltpu.make_async_remote_copy(
            src, dst, xs.at[k], xr.at[k], device_id=(to, me), device_id_type=MESH
        )

    first_half, second_half = pl.ds(0, half_rows), pl.ds(half_rows, half_rows)
    hops = [
        block_copy(civ_ref, blk_ref.at[0], 0, right),
        block_copy(civ_ref, blk_ref.at[1], 1, left),
        block_copy(blk_ref.at[0, first_half], blk_ref.at[2, first_half], 2, right),
        block_copy(blk_ref.at[1, second_half], blk_ref.at[2, second_half], 3, left),
    ]
    if groups == 2:
        hops = hops[:1]
    for hop in hops[:2]:
        hop.start()
    table[me] = rows_s[...]

    for block in blocks[early:]:
        invert(*block)

    line_ref[...] = jnp.zeros_like(line_ref)
    line_ref[0:1, 0:pairs] = h_ref[...].reshape(1, pairs)
    strips = [jnp.broadcast_to(line_ref[0:1, k * LANES : (k + 1) * LANES], (8, LANES)) for k in range(3)]

    def h_of(index):
        low = jnp.bitwise_and(index, 127)
        high = lax.shift_right_logical(index, 7)
        out = jnp.zeros(index.shape, F32)
        for k in range(3):
            out = jnp.where(high == k, lanes_of(strips[k], low), out)
        return out

    def h_step(i, c):
        start = pl.multiple_of(8 * i, 8)
        for lt in range(cuts):
            hx_ref[lt, pl.ds(start, 8), :] = h_of(pair_ref[lt, pl.ds(start, 8), :])
        return c

    lax.fori_loop(0, slots_deep // 8, h_step, 0)

    s_row = packed_row(
        wide_ref, exc_ref[0, pl.ds(2 * ga, 1), :].astype(F32), exc_ref[0, pl.ds(2 * ga + 1, 1), :].astype(F32), slots,
        batch_ref[2 * ga].astype(F32), batch_ref[2 * ga + 1].astype(F32),
    )
    g_row = packed_row(
        wide_ref, exc_ref[2, pl.ds(2 * ga, 1), :].astype(F32), exc_ref[2, pl.ds(2 * ga + 1, 1), :].astype(F32), slots, 1.0, 1.0
    )
    p_row = packed_row(
        wide_ref, exc_ref[1, pl.ds(2 * ga, 1), :].astype(F32), exc_ref[1, pl.ds(2 * ga + 1, 1), :].astype(F32), slots,
        float(EMPTY), float(EMPTY),
    )
    wide_lane = lax.broadcasted_iota(I32, (1, 2 * LANES), 1)
    g_row = jnp.where(wide_lane < 2 * string, g_row, 0.0)
    h_row = jnp.concatenate(
        [h_of(jnp.broadcast_to(p_row[:, k : k + LANES], (8, LANES)).astype(I32))[0:1] for k in (0, LANES)], axis=1
    )
    meta = jnp.concatenate(
        [s_row, g_row, jnp.where(wide_lane < string, h_row, 0.0), jnp.where(wide_lane < string, 0.0, h_row),
         jnp.zeros((4, 2 * LANES), F32)], axis=0
    ).T[0:ROWS]
    source, sign = meta[:, 0:1], meta[:, 1:2]

    def choose(block, owner):
        ids = (lax.broadcasted_iota(I32, (ROWS, rows_dev), 1) + owner * rows_dev).astype(F32)
        pick = jnp.where(source == ids, sign, 0.0).astype(BF16)
        parts2 = split(block)
        return dot(pick, parts2[0], NN), dot(pick, parts2[1], NN)

    a_high, a_low = choose(civ_ref[...], ga)

    def arrive(j):
        for b in range(2):
            for t in range(cuts):
                line = table[j, b * cuts + t : b * cuts + t + 1, :]
                texp[b, cuts * j + t] = jnp.broadcast_to(line, (8, LANES))
                t_ref[b, pl.ds(cuts * j + t, 1), :] = line

    def finish_row(d, c):
        j = lax.rem(me + d, parts)
        row_copy(j, j).wait_recv()
        arrive(j)
        return c

    arrive(me)
    lax.fori_loop(1, parts, finish_row, 0)

    total_rows = parts * cuts
    chunk = 24
    halves = split(jnp.concatenate([t_ref[0], t_ref[1]], axis=0))
    full = jnp.concatenate(halves, axis=1)

    def mux(got, high):
        for bit in range(3):
            n = got.shape[0] // 2
            got = got.reshape(n, 2, 8, LANES)
            mask = jnp.broadcast_to(jnp.bitwise_and(high, 1 << bit)[None], (n, 8, LANES)) != 0
            got = jnp.where(mask, got[:, 1], got[:, 0])
        return got

    sub = lax.broadcasted_iota(I32, (8, LANES), 0)
    tall = lax.broadcasted_iota(I32, (LANES, LANES), 0)

    def look_up(i, c):
        start = pl.multiple_of(8 * i, 8)
        for lt in range(cuts):
            src = look_ref[lt, pl.ds(start, 8), :]
            low = jnp.bitwise_and(src, 127)
            high = lax.shift_right_logical(src, 7)
            acc = [jnp.zeros((8, LANES), F32)] * 2
            if lt == 0:
                group = lax.shift_right_logical(high, 3)
                index = jnp.broadcast_to(low[None], (chunk, 8, LANES)).reshape(chunk * 8, LANES)
                for base in range(0, total_rows, chunk):
                    for b in range(2):
                        got = texp[b, base : base + chunk].reshape(chunk * 8, LANES)
                        got = mux(lanes_of(got, index).reshape(chunk, 8, LANES), high)
                        for k in range(chunk // 8):
                            acc[b] = jnp.where(group == base // 8 + k, got[k], acc[b])
            else:
                for r in range(0, 8, 2):
                    hot = jnp.concatenate(
                        [(tall == low[r + k : r + k + 1]).astype(F32).astype(BF16) for k in range(2)], axis=1
                    )
                    found = dot(full, jnp.concatenate([hot, hot], axis=0), NN)
                    for k in range(2):
                        wide = jnp.broadcast_to(high[r + k : r + k + 1], (8, LANES))
                        near = jnp.bitwise_and(wide, 7) == sub
                        group = lax.shift_right_logical(wide, 3)
                        for b in range(2):
                            mine = found[b * total_rows : (b + 1) * total_rows, k * LANES : (k + 1) * LANES]
                            mine = mine.reshape(total_rows // 8, 8, LANES)
                            best = mine[0]
                            for q in range(1, total_rows // 8):
                                best = jnp.where(group == q, mine[q], best)
                            value = jnp.sum(jnp.where(near, best, 0.0), axis=0, keepdims=True)
                            acc[b] = jnp.where(sub == r + k, value, acc[b])
            factor = sign_ref[lt, pl.ds(start, 8), :]
            vals_ref[0, lt, pl.ds(start, 8), :] = acc[0] * factor
            vals_ref[1, lt, pl.ds(start, 8), :] = acc[1] * factor
        return c

    tiles = slots_deep // 8
    relay = tiles // 2
    lax.fori_loop(0, relay, look_up, 0)
    for hop in hops[:2]:
        hop.wait_recv()
    for hop in hops[2:]:
        hop.start()
    lax.fori_loop(relay, tiles, look_up, 0)

    blank = jnp.zeros((LANES - slots_deep, LANES), F32)
    d2 = []
    for b in range(2):
        by_slot = jnp.concatenate(
            [jnp.concatenate([vals_ref[b, lt], blank], axis=0).T for lt in range(cuts)], axis=0
        )
        d2.append(split(jnp.concatenate(
            [lanes_of(by_slot, inv_ref[:, base : base + LANES]) for base in range(0, deep, LANES)], axis=1
        )))

    for hop in hops[2:]:
        hop.wait_recv()
    owners = [lax.rem(ga + groups - 1, groups), lax.rem(ga + 1, groups), lax.rem(ga + 2, groups)]
    for k in range(groups - 1):
        more = choose(blk_ref[k], owners[k])
        a_high, a_low = a_high + more[0], a_low + more[1]
    a2 = (a_high.astype(BF16), a_low.astype(BF16))
    a = a_high + a_low

    for b in range(2):
        from_a = jnp.sum(a * meta[:, 2 + b : 3 + b], axis=0, keepdims=True)
        for lt in range(cuts):
            cut = slice(lt * LANES, (lt + 1) * LANES)
            from_b = jnp.sum(vals_ref[b, lt] * hx_ref[lt], axis=0, keepdims=True)
            sigma_ref[b : b + 1, cut] = from_a[:, cut] + from_b

    def times(left, right, dims):
        n = left[0].shape[0]
        both = dot(jnp.concatenate(left, axis=0), right[0], dims)
        return (both[:n] + both[n:]) + dot(left[0], right[1], dims)

    row = lax.broadcasted_iota(I32, (ROWS, 1), 0)
    first = row < string
    low_rows, high_rows = 96, 80
    m0 = times(tuple(p[:low_rows] for p in a2), d2[0], NN)
    m1 = times(tuple(p[high_rows:] for p in a2), d2[1], NN)
    m = jnp.where(
        first,
        jnp.concatenate([m0, jnp.zeros((ROWS - low_rows, deep), F32)], axis=0),
        jnp.concatenate([jnp.zeros((high_rows, deep), F32), m1], axis=0),
    )
    gram = times(a2, a2, NT)
    gram = jnp.concatenate([gram, jnp.zeros((ROWS, 2 * LANES - ROWS), F32)], axis=1)
    gram = jnp.where(first, gram, pltpu.roll(gram, 2 * LANES - string, 1))
    again = pltpu.roll(gram, string, 1)[:, 0:LANES]
    lane = lax.broadcasted_iota(I32, (ROWS, LANES), 1)
    gram = jnp.where(lane < string, gram[:, 0:LANES], again)
    local = jnp.where(first, row, row - string)
    folded = barrel(gram, lax.rem(SHIFT - local + 2 * LANES, LANES), 7)
    last = jnp.where(lane < SHIFT, m[:, 2 * LANES :], jnp.where(lane < SHIFT + HALF, folded, 0.0))
    for rg in range(ROWS // 8):
        for lt in range(3):
            k = rg * 3 + lt
            piece = last if lt == 2 else m[:, lt * LANES : (lt + 1) * LANES]
            tiles_ref[k // per, k % per] = piece[8 * rg : 8 * rg + 8]
    tiles_ref[parts - 1, per - 1] = jnp.zeros((8, LANES), F32)

    def part_copy(j, slot):
        return pltpu.make_async_remote_copy(
            tiles_ref.at[j], got_ref.at[slot], ssem.at[j], rsem.at[slot], device_id=(ga, j), device_id_type=MESH
        )

    def send(d, c):
        part_copy(lax.rem(me + d, parts), me).start()
        return c

    lax.fori_loop(1, parts, send, 0)
    got_ref[me] = tiles_ref[me]

    def finish(d, c):
        j = lax.rem(me + d, parts)
        part_copy(j, j).wait_recv()
        return c

    lax.fori_loop(1, parts, finish, 0)
    zbuf[z] = jnp.sum(got_ref[...], axis=0)

    def z_copy(zz, slot):
        return pltpu.make_async_remote_copy(
            zbuf.at[slot], zbuf.at[slot], zs.at[zz], zr.at[slot], device_id=(ga, at(zz, y, core)), device_id_type=MESH
        )

    for k in range(1, nz):
        z_copy(lax.rem(z + k, nz), z).start()
    for k in range(1, nz):
        zz = lax.rem(z + k, nz)
        z_copy(zz, zz).wait_recv()

    def plane_copy(src, aa, yy, slot_a, slot_y):
        return pltpu.make_async_remote_copy(
            src, gat.at[slot_a, slot_y, core], fs.at[aa, yy], fr.at[slot_a, slot_y],
            device_id=(aa, at(z, yy, core)), device_id_type=MESH,
        )

    def twin_copy(src, slot_a, slot_y, slot_c):
        return pltpu.make_async_remote_copy(
            src, gat.at[slot_a, slot_y, slot_c], cs.at[slot_a, slot_y], cr.at[slot_a, slot_y],
            device_id=(ga, at(z, y, 1 - core)), device_id_type=MESH,
        )

    for aa, yy, _ in around:
        plane_copy(zbuf, aa, yy, ga, y).start()
    twin_copy(zbuf, ga, y, core).start()
    gat[ga, y, core] = zbuf[...]
    for aa, yy, _ in around:
        plane_copy(zbuf, aa, yy, aa, yy).wait_recv()
        twin_copy(gat.at[aa, yy, core], aa, yy, core).start()
    for aa, yy, _ in [(ga, y, 0)] + around:
        twin_copy(zbuf, aa, yy, 1 - core).wait_recv()

    def drain(d, c):
        j = lax.rem(me + d, parts)
        part_copy(j, j).wait_send()
        row_copy(j, j).wait_send()
        return c

    lax.fori_loop(1, parts, drain, 0)
    for hop in hops:
        hop.wait_send()
    for k in range(1, nz):
        z_copy(lax.rem(z + k, nz), z).wait_send()
    for aa, yy, _ in around:
        plane_copy(zbuf, aa, yy, ga, y).wait_send()
    for aa, yy, _ in [(ga, y, 0)] + around:
        twin_copy(zbuf, aa, yy, core).wait_send()


def place_kernel(groups, shape, slots, pairs, norm, exc_ref, gat, sigma_in, sigma_ref, density_ref, same_ref, mixed_ref,
                 r_ref, wide_ref):
    nz, ny, nc = shape
    per = 64 // (nz * ny * nc)
    string = slots + 1
    deep = 3 * LANES
    sigma_ref[...] = sigma_in[...]
    row = lax.broadcasted_iota(I32, (ROWS, 1), 0)
    first = row < string
    local = jnp.where(first, row, row - string)
    amount = lax.rem(local - SHIFT + 2 * LANES, LANES)
    lane = lax.broadcasted_iota(I32, (ROWS, LANES), 1)
    weights = jnp.where((lane == SHIFT) | (lane == SHIFT + HALF - 1), 0.5, 1.0)
    weights = jnp.where((lane >= SHIFT) & (lane < SHIFT + HALF), weights, 0.0)
    strip = lax.broadcasted_iota(I32, (1, LANES), 1)
    mixed = jnp.zeros((deep, deep), F32)
    upper = jnp.zeros((deep, deep), F32)
    for g in range(groups):
        for rg in range(ROWS // 8):
            for lt in range(3):
                k = rg * 3 + lt
                j, s = k // per, k % per
                r_ref[8 * rg : 8 * rg + 8, lt * LANES : (lt + 1) * LANES] = gat[
                    g, (j // nc) % ny, j % nc, j // (ny * nc), s
                ]
        ids = exc_ref[1, 2 * g : 2 * g + 2, :].astype(F32)
        p_row = packed_row(wide_ref, ids[0:1], ids[1:2], slots, float(pairs), float(pairs))
        placing = (lax.broadcasted_iota(I32, (deep, ROWS), 0).astype(F32) == p_row[:, 0:ROWS]).astype(BF16)
        mixed = mixed + dot2(placing, split(r_ref[...]), NN)
        half = barrel(r_ref[:, 2 * LANES :] * weights, amount, 7)
        both = jnp.concatenate([jnp.where(first, half, 0.0), jnp.where(first, 0.0, half)], axis=1)
        ends = []
        for b in range(2):
            line = wide_ref[b : b + 1, :]
            again = pltpu.roll(line, string, 1)
            line = jnp.where(strip < slots, line, jnp.where(strip == slots, float(pairs), again))
            ends.append(line)
        ext = jnp.concatenate(ends, axis=1)
        right = (lax.broadcasted_iota(I32, (deep, 2 * LANES), 0).astype(F32) == ext).astype(BF16)
        t = sum(dot(p, right, NT) for p in split(both))
        upper = upper + dot2(placing, split(t), NN)
    root = math.sqrt(norm)
    same = upper + upper.T
    density_ref[0:1, :] = same[pairs : pairs + 1, 0:pairs] * (1.0 / root)
    density_ref[1:2, :] = mixed[pairs : pairs + 1, 0:pairs] * (1.0 / root)
    same_ref[...] = same[0:pairs, 0:pairs] * (1.0 / norm)
    mixed_ref[...] = mixed[0:pairs, 0:pairs] * (1.0 / root)


def body(shape, civec, batch_index, exc_alpha, exc_beta, one_body):
    vmem = pl.BlockSpec(memory_space=pltpu.VMEM)
    smem = pl.BlockSpec(memory_space=pltpu.SMEM)
    nz, ny, nc = shape
    parts = nz * ny * nc
    per = 64 // parts
    groups = lax.axis_size("alpha")
    rows_dev, width = civec.shape
    total = batch_index.shape[0]
    batch = total // groups
    slots = exc_alpha.shape[2]
    pairs = one_body.shape[0]
    deep = 3 * LANES
    cuts = width // LANES
    slots_deep = -(-slots // 8) * 8
    dma = pltpu.SemaphoreType.DMA
    sigma, gat = pl.pallas_call(
        functools.partial(main_kernel, groups, shape, slots, pairs),
        out_shape=(
            jax.ShapeDtypeStruct((batch, width), F32),
            jax.ShapeDtypeStruct((groups, ny, nc, nz, per, 8, LANES), F32),
        ),
        in_specs=[smem, vmem, vmem, vmem, vmem],
        out_specs=(vmem, vmem),
        scratch_shapes=[
            pltpu.VMEM((cuts, slots_deep, LANES), I32),
            pltpu.VMEM((cuts, slots_deep, LANES), I32),
            pltpu.VMEM((cuts, slots_deep, LANES), F32),
            pltpu.VMEM((cuts, slots_deep, LANES), F32),
            pltpu.VMEM((width, deep), I32),
            pltpu.VMEM((2 * cuts, LANES), F32),
            pltpu.VMEM((parts, 2 * cuts, LANES), F32),
            pltpu.VMEM((2, parts * cuts, 8, LANES), F32),
            pltpu.VMEM((2, parts * cuts, LANES), F32),
            pltpu.VMEM((2, cuts, slots_deep, LANES), F32),
            pltpu.VMEM((max(groups - 1, 2), rows_dev, width), F32),
            pltpu.VMEM((8, deep), F32),
            pltpu.VMEM((8, LANES), F32),
            pltpu.VMEM((parts, per, 8, LANES), F32),
            pltpu.VMEM((parts, per, 8, LANES), F32),
            pltpu.VMEM((nz, per, 8, LANES), F32),
            dma((parts,)), dma((parts,)),
            dma((4,)), dma((4,)),
            dma((parts,)), dma((parts,)),
            dma((nz,)), dma((nz,)),
            dma((groups, ny)), dma((groups, ny)),
            dma((groups, ny)), dma((groups, ny)),
        ],
        compiler_params=pltpu.CompilerParams(collective_id=0, has_side_effects=True),
        name="main",
    )(batch_index, exc_alpha, exc_beta.swapaxes(1, 2), one_body, civec)
    return tuple(pl.pallas_call(
        functools.partial(place_kernel, groups, shape, slots, pairs, total * width * parts),
        out_shape=(
            jax.ShapeDtypeStruct((batch, width), F32),
            jax.ShapeDtypeStruct((2, pairs), F32),
            jax.ShapeDtypeStruct((pairs, pairs), F32),
            jax.ShapeDtypeStruct((pairs, pairs), F32),
        ),
        in_specs=[vmem, vmem, vmem],
        out_specs=(vmem, vmem, vmem, vmem),
        scratch_shapes=[pltpu.VMEM((ROWS, deep), F32), pltpu.VMEM((8, LANES), F32)],
        name="place",
    )(exc_alpha, gat, sigma))


def solution(mesh, shape=(8, 4, 2)):
    in_specs = (P("alpha", "beta"), P(), P(), P(None, "beta", None), P())
    out_specs = (P("alpha", "beta"), P(), P(), P())
    return jax.shard_map(
        functools.partial(body, shape), mesh=mesh, in_specs=in_specs, out_specs=out_specs, check_vma=False
    )
```

```python
import functools
import math

import jax
import jax.numpy as jnp
from jax import lax
from jax.experimental import pallas as pl
from jax.experimental.pallas import tpu as pltpu
from jax.sharding import PartitionSpec as P

MESH = pl.DeviceIdType.MESH
F32, BF16, I32 = jnp.float32, jnp.bfloat16, jnp.int32
LANES = 128
HALF = 42
SHIFT = 68
ROWS = 168
EMPTY = 511
NT = (((1,), (1,)), ((), ()))
NN = (((1,), (0,)), ((), ()))
ALONG = lax.GatherDimensionNumbers(
    offset_dims=(), collapsed_slice_dims=(1,), start_index_map=(1,), operand_batching_dims=(0,), start_indices_batching_dims=(0,)
)


def split(x):
    high = x.astype(BF16)
    return high, (x - high.astype(F32)).astype(BF16)


def dot(a, b, dims):
    return lax.dot_general(a, b, dims, preferred_element_type=F32)


def dot3(a, b, dims):
    return dot(a[0], b[0], dims) + (dot(a[0], b[1], dims) + dot(a[1], b[0], dims))


def dot2(a, b, dims):
    return dot(a, b[0], dims) + dot(a, b[1], dims)


def lanes_of(x, index):
    return lax.gather(x, index[..., None], ALONG, (1, 1), mode=lax.GatherScatterMode.PROMISE_IN_BOUNDS)


def barrel(x, amount, bits):
    for bit in range(bits):
        moved = pltpu.roll(x, 1 << bit, 1)
        x = jnp.where(lax.rem(lax.div(amount, 1 << bit), 2) == 1, moved, x)
    return x


def packed_row(wide_ref, first, second, slots, end_first, end_second):
    string = slots + 1
    wide_ref[...] = jnp.zeros_like(wide_ref)
    wide_ref[0:1, 0:slots] = first
    wide_ref[1:2, 0:slots] = second
    lane = lax.broadcasted_iota(I32, (1, 2 * LANES), 1)
    blank = jnp.zeros((1, LANES), F32)
    one = jnp.concatenate([wide_ref[0:1, :], blank], axis=1)
    two = pltpu.roll(jnp.concatenate([wide_ref[1:2, :], blank], axis=1), string, 1)
    out = jnp.where(lane < string, one, two)
    out = jnp.where(lane == slots, end_first, jnp.where(lane == string + slots, end_second, out))
    return jnp.where(lane < 2 * string, out, float(EMPTY))


def main_kernel(groups, shape, slots, pairs, batch_ref, exc_ref, beta_ref, h_ref, civ_ref, sigma_ref, gat,
                pair_ref, look_ref, sign_ref, hx_ref, inv_ref, rows_s, table, texp, t_ref, vals_ref, blk_ref, line_ref,
                wide_ref, tiles_ref, pair_buf, sums, got_ref, zbuf, dummy,
                ts, tr, xs, xr, ps, pr, ssem, rsem, zs, zr, fs, fr, cs, cr):
    nz, ny, nc = shape
    parts = nz * ny * nc
    per = 64 // parts
    width = beta_ref.shape[2]
    cuts = width // LANES
    deep = 3 * LANES
    slots_deep = look_ref.shape[1]
    rows_dev = civ_ref.shape[0]
    string = slots + 1
    ga = lax.axis_index("alpha")
    me = lax.axis_index("beta")
    z, y, core = me // (ny * nc), (me // nc) % ny, me % nc
    planes = groups * ny

    def at(zz, yy, cc):
        return (zz * ny + yy) * nc + cc

    barrier = pltpu.get_barrier_semaphore()
    others = parts - 1
    burst = 7 if others % 7 == 0 else 1

    def far_first(k):
        return lax.rem(me + 1 + lax.rem(k + (others * 5) // 16, others), parts)

    def each(action):
        def step(k, c):
            for i in range(burst):
                action(far_first(burst * k + i))
            return c

        lax.fori_loop(0, others // burst, step, 0)

    each(lambda j: pl.semaphore_signal(barrier, inc=1, device_id=(ga, j), device_id_type=MESH))

    def spread_of(k):
        return min(k // ny, groups - k // ny) + min(k % ny, ny - k % ny)

    near = sorted(range(1, planes), key=spread_of)
    around = [(lax.rem(ga + k // ny, groups), lax.rem(y + k % ny, ny), k // ny) for k in near]
    extra = 0
    for aa, yy, off in around:
        if off:
            pl.semaphore_signal(barrier, inc=1, device_id=(aa, at(z, yy, core)), device_id_type=MESH)
            extra += 1
    for b in range(2):
        row = civ_ref[pl.ds(lax.rem(batch_ref[2 * ga + b], rows_dev), 1), :]
        for t in range(cuts):
            rows_s[b * cuts + t : b * cuts + t + 1, :] = row[:, t * LANES : (t + 1) * LANES]

    last_tile = slots_deep - 8
    for lt in range(cuts):
        cut = slice(lt * LANES, (lt + 1) * LANES)
        pair_ref[lt, last_tile:, :] = jnp.full((8, LANES), EMPTY, I32)
        look_ref[lt, last_tile:, :] = jnp.zeros((8, LANES), I32)
        sign_ref[lt, last_tile:, :] = jnp.zeros((8, LANES), F32)
        look_ref[lt, 0:slots, :] = beta_ref[0, :, cut]
        pair_ref[lt, 0:slots, :] = beta_ref[1, :, cut]
        sign_ref[lt, 0:slots, :] = beta_ref[2, :, cut].astype(F32)

    blocks = [(lt, base) for base in range(0, pairs, LANES) for lt in range(cuts)]

    def invert(lt, base):
        size = min(LANES, -(-(pairs - base) // 8) * 8)
        ids = lax.broadcasted_iota(I32, (size, LANES), 0) + base

        def mark(e, acc):
            for k in range(9):
                acc = jnp.where(pair_ref[lt, pl.ds(9 * e + k, 1), :] == ids, 9 * e + k, acc)
            return acc

        acc = lax.fori_loop(0, slots // 9, mark, jnp.full((size, LANES), LANES - 1, I32))
        if size < LANES:
            acc = jnp.concatenate([acc, jnp.full((LANES - size, LANES), LANES - 1, I32)], axis=0)
        inv_ref[lt * LANES : (lt + 1) * LANES, base : base + LANES] = acc.T

    early = len(blocks) // 2
    for block in blocks[:early]:
        invert(*block)

    pl.semaphore_wait(barrier, parts - 1 + extra)

    def row_copy(j, slot):
        return pltpu.make_async_remote_copy(
            rows_s, table.at[slot], ts.at[j], tr.at[slot], device_id=(ga, j), device_id_type=MESH
        )

    each(lambda j: row_copy(j, me).start())

    right, left = lax.rem(ga + 1, groups), lax.rem(ga + groups - 1, groups)
    half_rows = rows_dev // 2

    def block_copy(src, dst, k, to):
        return pltpu.make_async_remote_copy(
            src, dst, xs.at[k], xr.at[k], device_id=(to, me), device_id_type=MESH
        )

    first_half, second_half = pl.ds(0, half_rows), pl.ds(half_rows, half_rows)
    hops = [
        block_copy(civ_ref, blk_ref.at[0], 0, right),
        block_copy(civ_ref, blk_ref.at[1], 1, left),
        block_copy(blk_ref.at[0, first_half], blk_ref.at[2, first_half], 2, right),
        block_copy(blk_ref.at[1, second_half], blk_ref.at[2, second_half], 3, left),
    ]
    if groups == 2:
        hops = hops[:1]
    for hop in hops[:2]:
        hop.start()
    table[me] = rows_s[...]

    for block in blocks[early:]:
        invert(*block)

    line_ref[...] = jnp.zeros_like(line_ref)
    line_ref[0:1, 0:pairs] = h_ref[...].reshape(1, pairs)
    strips = [jnp.broadcast_to(line_ref[0:1, k * LANES : (k + 1) * LANES], (8, LANES)) for k in range(3)]

    def h_of(index):
        low = jnp.bitwise_and(index, 127)
        high = lax.shift_right_logical(index, 7)
        out = jnp.zeros(index.shape, F32)
        for k in range(3):
            out = jnp.where(high == k, lanes_of(strips[k], low), out)
        return out

    def h_step(i, c):
        start = pl.multiple_of(8 * i, 8)
        for lt in range(cuts):
            hx_ref[lt, pl.ds(start, 8), :] = h_of(pair_ref[lt, pl.ds(start, 8), :])
        return c

    lax.fori_loop(0, slots_deep // 8, h_step, 0)

    s_row = packed_row(
        wide_ref, exc_ref[0, pl.ds(2 * ga, 1), :].astype(F32), exc_ref[0, pl.ds(2 * ga + 1, 1), :].astype(F32), slots,
        batch_ref[2 * ga].astype(F32), batch_ref[2 * ga + 1].astype(F32),
    )
    g_row = packed_row(
        wide_ref, exc_ref[2, pl.ds(2 * ga, 1), :].astype(F32), exc_ref[2, pl.ds(2 * ga + 1, 1), :].astype(F32), slots, 1.0, 1.0
    )
    p_row = packed_row(
        wide_ref, exc_ref[1, pl.ds(2 * ga, 1), :].astype(F32), exc_ref[1, pl.ds(2 * ga + 1, 1), :].astype(F32), slots,
        float(EMPTY), float(EMPTY),
    )
    wide_lane = lax.broadcasted_iota(I32, (1, 2 * LANES), 1)
    g_row = jnp.where(wide_lane < 2 * string, g_row, 0.0)
    h_row = jnp.concatenate(
        [h_of(jnp.broadcast_to(p_row[:, k : k + LANES], (8, LANES)).astype(I32))[0:1] for k in (0, LANES)], axis=1
    )
    meta = jnp.concatenate(
        [s_row, g_row, jnp.where(wide_lane < string, h_row, 0.0), jnp.where(wide_lane < string, 0.0, h_row),
         jnp.zeros((4, 2 * LANES), F32)], axis=0
    ).T[0:ROWS]
    source, sign = meta[:, 0:1], meta[:, 1:2]

    def choose(block, owner):
        ids = (lax.broadcasted_iota(I32, (ROWS, rows_dev), 1) + owner * rows_dev).astype(F32)
        pick = jnp.where(source == ids, sign, 0.0).astype(BF16)
        parts2 = split(block)
        return dot(pick, parts2[0], NN), dot(pick, parts2[1], NN)

    a_high, a_low = choose(civ_ref[...], ga)

    def arrive(j):
        for b in range(2):
            for t in range(cuts):
                line = table[j, b * cuts + t : b * cuts + t + 1, :]
                texp[b, cuts * j + t] = jnp.broadcast_to(line, (8, LANES))
                t_ref[b, pl.ds(cuts * j + t, 1), :] = line

    def finish_row(d, c):
        j = lax.rem(me + d, parts)
        row_copy(j, j).wait_recv()
        arrive(j)
        return c

    arrive(me)
    lax.fori_loop(1, parts, finish_row, 0)

    total_rows = parts * cuts
    chunk = 24
    halves = split(jnp.concatenate([t_ref[0], t_ref[1]], axis=0))
    full = jnp.concatenate(halves, axis=1)

    levels = 3 if total_rows % 64 == 0 else 0

    def mux(got, high, low_bit, count):
        for bit in range(low_bit, low_bit + count):
            n = got.shape[0] // 2
            got = got.reshape(n, 2, 8, LANES)
            mask = jnp.broadcast_to(jnp.bitwise_and(high, 1 << bit)[None], (n, 8, LANES)) != 0
            got = jnp.where(mask, got[:, 1], got[:, 0])
        return got

    sub = lax.broadcasted_iota(I32, (8, LANES), 0)
    tall = lax.broadcasted_iota(I32, (LANES, LANES), 0).astype(F32).astype(BF16)
    blank_hot, full_hot = jnp.zeros((LANES, LANES), BF16), jnp.ones((LANES, LANES), BF16)

    def look_up(i):
        start = pl.multiple_of(8 * i, 8)
        for lt in range(cuts):
            src = look_ref[lt, pl.ds(start, 8), :]
            low = jnp.bitwise_and(src, 127)
            high = lax.shift_right_logical(src, 7)
            acc = [jnp.zeros((8, LANES), F32)] * 2
            if lt == 0:
                group = lax.shift_right_logical(high, 3)
                index = jnp.broadcast_to(low[None], (chunk, 8, LANES)).reshape(chunk * 8, LANES)
                for base in range(0, total_rows, chunk):
                    for b in range(2):
                        got = texp[b, base : base + chunk].reshape(chunk * 8, LANES)
                        got = mux(lanes_of(got, index).reshape(chunk, 8, LANES), high, 0, 3)
                        for k in range(chunk // 8):
                            acc[b] = jnp.where(group == base // 8 + k, got[k], acc[b])
            else:
                for r in range(0, 8, 2):
                    hot = []
                    for k in range(2):
                        line = jnp.broadcast_to(low[r + k : r + k + 1], (16, LANES)).astype(F32).astype(BF16)
                        hot.append(jnp.where(tall == jnp.concatenate([line] * 8, axis=0), full_hot, blank_hot))
                    hot = jnp.concatenate(hot, axis=1)
                    found = dot(full, jnp.concatenate([hot, hot], axis=0), NN)
                    for k in range(2):
                        wide = jnp.broadcast_to(high[r + k : r + k + 1], (8, LANES))
                        near = jnp.bitwise_and(wide, 7) == sub
                        block = lax.shift_right_logical(wide, 3 + levels)
                        for b in range(2):
                            mine = found[b * total_rows : (b + 1) * total_rows, k * LANES : (k + 1) * LANES]
                            mine = mux(mine.reshape(total_rows // 8, 8, LANES), wide, 3, levels)
                            best = mine[0]
                            for q in range(1, mine.shape[0]):
                                best = jnp.where(block == q, mine[q], best)
                            value = jnp.sum(jnp.where(near, best, 0.0), axis=0, keepdims=True)
                            acc[b] = jnp.where(sub == r + k, value, acc[b])
            factor = sign_ref[lt, pl.ds(start, 8), :]
            vals_ref[0, lt, pl.ds(start, 8), :] = acc[0] * factor
            vals_ref[1, lt, pl.ds(start, 8), :] = acc[1] * factor

    def look_two(i, c):
        look_up(2 * i)
        look_up(2 * i + 1)
        return c

    tiles = slots_deep // 8
    relay = tiles // 4
    lax.fori_loop(0, relay, look_two, 0)
    for hop in hops[:2]:
        hop.wait_recv()
    for hop in hops[2:]:
        hop.start()
    lax.fori_loop(relay, tiles // 2, look_two, 0)
    for i in range(tiles // 2 * 2, tiles):
        look_up(i)
    for hop in hops[2:]:
        hop.wait_recv()

    blank = jnp.zeros((LANES - slots_deep, LANES), F32)
    d2 = []
    for b in range(2):
        by_slot = jnp.concatenate(
            [jnp.concatenate([vals_ref[b, lt], blank], axis=0).T for lt in range(cuts)], axis=0
        )
        d2.append(split(jnp.concatenate(
            [lanes_of(by_slot, inv_ref[:, base : base + LANES]) for base in range(0, deep, LANES)], axis=1
        )))

    owners = [lax.rem(ga + groups - 1, groups), lax.rem(ga + 1, groups), lax.rem(ga + 2, groups)]
    for k in range(groups - 1):
        more = choose(blk_ref[k], owners[k])
        a_high, a_low = a_high + more[0], a_low + more[1]
    a2 = (a_high.astype(BF16), a_low.astype(BF16))
    a = a_high + a_low

    def times(left, right, dims):
        n = left[0].shape[0]
        both = dot(jnp.concatenate(left, axis=0), right[0], dims)
        return (both[:n] + both[n:]) + dot(left[0], right[1], dims)

    row = lax.broadcasted_iota(I32, (ROWS, 1), 0)
    first = row < string
    low_rows, high_rows = 96, 80
    m0 = times(tuple(p[:low_rows] for p in a2), d2[0], NN)
    m1 = times(tuple(p[high_rows:] for p in a2), d2[1], NN)
    m = jnp.where(
        first,
        jnp.concatenate([m0, jnp.zeros((ROWS - low_rows, deep), F32)], axis=0),
        jnp.concatenate([jnp.zeros((high_rows, deep), F32), m1], axis=0),
    )
    gram = times(a2, a2, NT)
    gram = jnp.concatenate([gram, jnp.zeros((ROWS, 2 * LANES - ROWS), F32)], axis=1)
    gram = jnp.where(first, gram, pltpu.roll(gram, 2 * LANES - string, 1))
    again = pltpu.roll(gram, string, 1)[:, 0:LANES]
    lane = lax.broadcasted_iota(I32, (ROWS, LANES), 1)
    gram = jnp.where(lane < string, gram[:, 0:LANES], again)
    local = jnp.where(first, row, row - string)
    folded = barrel(gram, lax.rem(SHIFT - local + 2 * LANES, LANES), 7)
    last = jnp.where(lane < SHIFT, m[:, 2 * LANES :], jnp.where(lane < SHIFT + HALF, folded, 0.0))
    for rg in range(ROWS // 8):
        for lt in range(3):
            k = rg * 3 + lt
            piece = last if lt == 2 else m[:, lt * LANES : (lt + 1) * LANES]
            tiles_ref[(k // per) % nc, k // per // nc, k % per] = piece[8 * rg : 8 * rg + 8]
    tiles_ref[nc - 1, parts // nc - 1, per - 1] = jnp.zeros((8, LANES), F32)

    def settled(count, sem):
        return pltpu.make_async_remote_copy(
            dummy.at[pl.ds(0, count)], dummy.at[pl.ds(0, count)], sem, sem, device_id=(right, me), device_id_type=MESH
        )

    chips = parts // nc
    chip = z * ny + y
    pair = pltpu.make_async_remote_copy(
        tiles_ref.at[1 - core], pair_buf, ps, pr, device_id=(ga, at(z, y, 1 - core)), device_id_type=MESH
    )
    pair.start()

    def drain_row(k, c):
        row_copy(far_first(k), me).wait_send()
        return c

    for b in range(2):
        from_a = jnp.sum(a * meta[:, 2 + b : 3 + b], axis=0, keepdims=True)
        for lt in range(cuts):
            cut = slice(lt * LANES, (lt + 1) * LANES)
            from_b = jnp.sum(vals_ref[b, lt] * hx_ref[lt], axis=0, keepdims=True)
            sigma_ref[b : b + 1, cut] = from_a[:, cut] + from_b
    pair.wait_recv()
    sums[...] = tiles_ref[core] + pair_buf[...]

    def part_copy(q):
        return pltpu.make_async_remote_copy(
            sums.at[q], got_ref.at[chip], ssem, rsem, device_id=(ga, q * nc + core), device_id_type=MESH
        )

    def send_part(k, c):
        part_copy(lax.rem(chip + 1 + lax.rem(k + (chips * 5) // 16, chips - 1), chips)).start()
        return c

    lax.fori_loop(0, chips - 1, send_part, 0)
    got_ref[chip] = sums[chip]
    lax.fori_loop(0, others, drain_row, 0)
    for hop in hops:
        hop.wait_send()
    pair.wait_send()
    settled((chips - 1) * per, rsem).wait_recv()
    zbuf[z] = jnp.sum(got_ref[...], axis=0)

    def z_copy(zz):
        return pltpu.make_async_remote_copy(
            zbuf.at[z], zbuf.at[z], zs, zr, device_id=(ga, at(zz, y, core)), device_id_type=MESH
        )

    for k in sorted(range(1, nz), key=lambda k: -min(k, nz - k)):
        z_copy(lax.rem(z + k, nz)).start()
    settled((chips - 1) * per, ssem).wait_send()
    if nz > 1:
        settled((nz - 1) * per, zr).wait_recv()

    def plane_copy(src, aa, yy, slot_a, slot_y):
        return pltpu.make_async_remote_copy(
            src, gat.at[slot_a, slot_y, core], fs, fr.at[slot_a, slot_y],
            device_id=(aa, at(z, yy, core)), device_id_type=MESH,
        )

    def twin_copy(src, slot_a, slot_y):
        return pltpu.make_async_remote_copy(
            src, gat.at[slot_a, slot_y, core], cs, cr,
            device_id=(ga, at(z, y, 1 - core)), device_id_type=MESH,
        )

    for aa, yy, _ in around[::-1]:
        plane_copy(zbuf, aa, yy, ga, y).start()
    twin_copy(zbuf, ga, y).start()
    gat[ga, y, core] = zbuf[...]
    for aa, yy, _ in around:
        plane_copy(zbuf, aa, yy, aa, yy).wait_recv()
        twin_copy(gat.at[aa, yy, core], aa, yy).start()
    if nz > 1:
        settled((nz - 1) * per, zs).wait_send()
    settled((planes - 1) * nz * per, fs).wait_send()
    settled(planes * nz * per, cr).wait_recv()
    settled(planes * nz * per, cs).wait_send()


def place_kernel(groups, shape, slots, pairs, norm, exc_ref, gat, sigma_in, sigma_ref, density_ref, same_ref, mixed_ref,
                 r_ref, t_ref, wide_ref):
    nz, ny, nc = shape
    per = 64 // (nz * ny * nc)
    string = slots + 1
    deep = 3 * LANES
    sigma_ref[...] = sigma_in[...]
    row = lax.broadcasted_iota(I32, (ROWS, 1), 0)
    first = row < string
    local = jnp.where(first, row, row - string)
    amount = lax.rem(local - SHIFT + 2 * LANES, LANES)
    lane = lax.broadcasted_iota(I32, (ROWS, LANES), 1)
    weights = jnp.where((lane == SHIFT) | (lane == SHIFT + HALF - 1), 0.5, 1.0)
    weights = jnp.where((lane >= SHIFT) & (lane < SHIFT + HALF), weights, 0.0)
    strip = lax.broadcasted_iota(I32, (1, LANES), 1)
    wide = lax.broadcasted_iota(I32, (1, 2 * LANES), 1)
    span = -(-groups * ROWS // LANES) * LANES
    p_all = jnp.zeros((1, span), F32)
    exts = []
    for g in range(groups):
        rows = slice(g * ROWS, (g + 1) * ROWS)
        for rg in range(ROWS // 8):
            for lt in range(3):
                k = rg * 3 + lt
                j, s = k // per, k % per
                r_ref[g * ROWS + 8 * rg : g * ROWS + 8 * rg + 8, lt * LANES : (lt + 1) * LANES] = gat[
                    g, (j // nc) % ny, j % nc, j // (ny * nc), s
                ]
        ids = exc_ref[1, 2 * g : 2 * g + 2, :].astype(F32)
        p_row = packed_row(wide_ref.at[g], ids[0:1], ids[1:2], slots, float(pairs), float(pairs))
        p_row = jnp.where(wide < ROWS, p_row, 0.0)
        p_row = jnp.concatenate([p_row, jnp.zeros((1, span - 2 * LANES), F32)], axis=1)
        p_all = p_all + (pltpu.roll(p_row, g * ROWS, 1) if g else p_row)
        ends = []
        for b in range(2):
            line = wide_ref[g, b : b + 1, :]
            again = pltpu.roll(line, string, 1)
            line = jnp.where(strip < slots, line, jnp.where(strip == slots, float(pairs), again))
            ends.append(line)
        exts.append(jnp.concatenate(ends, axis=1))
    exts = jnp.concatenate(exts + [jnp.zeros((8 - groups, 2 * LANES), F32)], axis=0).T
    for g in range(groups):
        rows = slice(g * ROWS, (g + 1) * ROWS)
        half = barrel(r_ref[rows, 2 * LANES :] * weights, amount, 7)
        both = split(jnp.concatenate([jnp.where(first, half, 0.0), jnp.where(first, 0.0, half)], axis=1))
        right = (lax.broadcasted_iota(I32, (2 * LANES, deep), 1).astype(F32) == exts[:, g : g + 1]).astype(BF16)
        twice = dot(jnp.concatenate(both, axis=0), right, NN)
        t_ref[rows, :] = twice[:ROWS] + twice[ROWS:]
    placing = (lax.broadcasted_iota(I32, (deep, groups * ROWS), 0).astype(F32) == p_all[:, : groups * ROWS]).astype(BF16)
    mixed = dot2(placing, split(r_ref[...]), NN)
    upper = dot2(placing, split(t_ref[...]), NN)
    root = math.sqrt(norm)
    same = upper + upper.T
    density_ref[0:1, :] = same[pairs : pairs + 1, 0:pairs] * (1.0 / root)
    density_ref[1:2, :] = mixed[pairs : pairs + 1, 0:pairs] * (1.0 / root)
    same_ref[...] = same[0:pairs, 0:pairs] * (1.0 / norm)
    mixed_ref[...] = mixed[0:pairs, 0:pairs] * (1.0 / root)


def body(shape, civec, batch_index, exc_alpha, exc_beta, one_body):
    vmem = pl.BlockSpec(memory_space=pltpu.VMEM)
    smem = pl.BlockSpec(memory_space=pltpu.SMEM)
    nz, ny, nc = shape
    parts = nz * ny * nc
    per = 64 // parts
    groups = lax.axis_size("alpha")
    rows_dev, width = civec.shape
    total = batch_index.shape[0]
    batch = total // groups
    slots = exc_alpha.shape[2]
    pairs = one_body.shape[0]
    deep = 3 * LANES
    cuts = width // LANES
    slots_deep = -(-slots // 8) * 8
    dma = pltpu.SemaphoreType.DMA
    sigma, gat = pl.pallas_call(
        functools.partial(main_kernel, groups, shape, slots, pairs),
        out_shape=(
            jax.ShapeDtypeStruct((batch, width), F32),
            jax.ShapeDtypeStruct((groups, ny, nc, nz, per, 8, LANES), F32),
        ),
        in_specs=[smem, vmem, vmem, vmem, vmem],
        out_specs=(vmem, vmem),
        scratch_shapes=[
            pltpu.VMEM((cuts, slots_deep, LANES), I32),
            pltpu.VMEM((cuts, slots_deep, LANES), I32),
            pltpu.VMEM((cuts, slots_deep, LANES), F32),
            pltpu.VMEM((cuts, slots_deep, LANES), F32),
            pltpu.VMEM((width, deep), I32),
            pltpu.VMEM((2 * cuts, LANES), F32),
            pltpu.VMEM((parts, 2 * cuts, LANES), F32),
            pltpu.VMEM((2, parts * cuts, 8, LANES), F32),
            pltpu.VMEM((2, parts * cuts, LANES), F32),
            pltpu.VMEM((2, cuts, slots_deep, LANES), F32),
            pltpu.VMEM((max(groups - 1, 2), rows_dev, width), F32),
            pltpu.VMEM((8, deep), F32),
            pltpu.VMEM((8, LANES), F32),
            pltpu.VMEM((nc, parts // nc, per, 8, LANES), F32),
            pltpu.VMEM((parts // nc, per, 8, LANES), F32),
            pltpu.VMEM((parts // nc, per, 8, LANES), F32),
            pltpu.VMEM((parts // nc, per, 8, LANES), F32),
            pltpu.VMEM((nz, per, 8, LANES), F32),
            pltpu.VMEM((groups * ny * nz * per, 8, LANES), F32),
            dma((parts,)), dma((parts,)),
            dma((4,)), dma((4,)),
            dma, dma, dma, dma, dma, dma, dma,
            dma((groups, ny)),
            dma, dma,
        ],
        compiler_params=pltpu.CompilerParams(collective_id=0, has_side_effects=True),
        name="main",
    )(batch_index, exc_alpha, exc_beta.swapaxes(1, 2), one_body, civec)
    return tuple(pl.pallas_call(
        functools.partial(place_kernel, groups, shape, slots, pairs, total * width * parts),
        out_shape=(
            jax.ShapeDtypeStruct((batch, width), F32),
            jax.ShapeDtypeStruct((2, pairs), F32),
            jax.ShapeDtypeStruct((pairs, pairs), F32),
            jax.ShapeDtypeStruct((pairs, pairs), F32),
        ),
        in_specs=[vmem, vmem, vmem],
        out_specs=(vmem, vmem, vmem, vmem),
        scratch_shapes=[pltpu.VMEM((groups * ROWS, deep), F32)] * 2 + [pltpu.VMEM((groups, 8, LANES), F32)],
        name="place",
    )(exc_alpha, gat, sigma))


def solution(mesh, shape=(8, 4, 2)):
    in_specs = (P("alpha", "beta"), P(), P(), P(None, "beta", None), P())
    out_specs = (P("alpha", "beta"), P(), P(), P())
    return jax.shard_map(
        functools.partial(body, shape), mesh=mesh, in_specs=in_specs, out_specs=out_specs, check_vma=False
    )
```

```python
import functools
import math

import jax
import jax.numpy as jnp
from jax import lax
from jax.experimental import pallas as pl
from jax.experimental.pallas import tpu as pltpu
from jax.sharding import PartitionSpec as P

MESH = pl.DeviceIdType.MESH
F32, BF16, I32 = jnp.float32, jnp.bfloat16, jnp.int32
LANES = 128
HALF = 42
SHIFT = 68
ROWS = 168
EMPTY = 511
NT = (((1,), (1,)), ((), ()))
NN = (((1,), (0,)), ((), ()))
ALONG = lax.GatherDimensionNumbers(
    offset_dims=(), collapsed_slice_dims=(1,), start_index_map=(1,), operand_batching_dims=(0,), start_indices_batching_dims=(0,)
)


def split(x):
    high = x.astype(BF16)
    return high, (x - high.astype(F32)).astype(BF16)


def dot(a, b, dims):
    return lax.dot_general(a, b, dims, preferred_element_type=F32)


def dot3(a, b, dims):
    return dot(a[0], b[0], dims) + (dot(a[0], b[1], dims) + dot(a[1], b[0], dims))


def dot2(a, b, dims):
    return dot(a, b[0], dims) + dot(a, b[1], dims)


def lanes_of(x, index):
    return lax.gather(x, index[..., None], ALONG, (1, 1), mode=lax.GatherScatterMode.PROMISE_IN_BOUNDS)


def barrel(x, amount, bits):
    for bit in range(bits):
        moved = pltpu.roll(x, 1 << bit, 1)
        x = jnp.where(lax.rem(lax.div(amount, 1 << bit), 2) == 1, moved, x)
    return x


def packed_row(wide_ref, first, second, slots, end_first, end_second):
    string = slots + 1
    wide_ref[...] = jnp.zeros_like(wide_ref)
    wide_ref[0:1, 0:slots] = first
    wide_ref[1:2, 0:slots] = second
    lane = lax.broadcasted_iota(I32, (1, 2 * LANES), 1)
    blank = jnp.zeros((1, LANES), F32)
    one = jnp.concatenate([wide_ref[0:1, :], blank], axis=1)
    two = pltpu.roll(jnp.concatenate([wide_ref[1:2, :], blank], axis=1), string, 1)
    out = jnp.where(lane < string, one, two)
    out = jnp.where(lane == slots, end_first, jnp.where(lane == string + slots, end_second, out))
    return jnp.where(lane < 2 * string, out, float(EMPTY))


def main_kernel(groups, shape, slots, pairs, batch_ref, exc_ref, beta_hbm, h_ref, civ_hbm, sigma_ref, gat,
                beta_ref, civ_ref, pair_ref, look_ref, sign_ref, hx_ref, inv_ref, rows_s, table, texp, t_ref, vals_ref, blk_ref, line_ref,
                wide_ref, tiles_ref, pair_buf, sums, got_ref, zbuf, dummy,
                in_sem, ts, tr, xs, xr, ps, pr, ssem, rsem, zs, zr, fs, fr, cs, cr):
    nz, ny, nc = shape
    parts = nz * ny * nc
    per = 64 // parts
    width = beta_ref.shape[2]
    cuts = width // LANES
    deep = 3 * LANES
    slots_deep = look_ref.shape[1]
    rows_dev = civ_ref.shape[0]
    string = slots + 1
    ga = lax.axis_index("alpha")
    me = lax.axis_index("beta")
    z, y, core = me // (ny * nc), (me // nc) % ny, me % nc
    planes = groups * ny

    def at(zz, yy, cc):
        return (zz * ny + yy) * nc + cc

    loads = [pltpu.make_async_copy(civ_hbm, civ_ref, in_sem.at[0]), pltpu.make_async_copy(beta_hbm, beta_ref, in_sem.at[1])]
    for load in loads:
        load.start()
    barrier = pltpu.get_barrier_semaphore()
    others = parts - 1
    burst = 7 if others % 7 == 0 else 1

    def far_first(k):
        return lax.rem(me + 1 + lax.rem(k + (others * 5) // 16, others), parts)

    def each(action):
        def step(k, c):
            for i in range(burst):
                action(far_first(burst * k + i))
            return c

        lax.fori_loop(0, others // burst, step, 0)

    each(lambda j: pl.semaphore_signal(barrier, inc=1, device_id=(ga, j), device_id_type=MESH))

    for d in range(1, groups):
        pl.semaphore_signal(barrier, inc=1, device_id=(lax.rem(ga + d, groups), me), device_id_type=MESH)
    extra = groups - 1

    for load in loads:
        load.wait()
    for b in range(2):
        row = civ_ref[pl.ds(lax.rem(batch_ref[2 * ga + b], rows_dev), 1), :]
        for t in range(cuts):
            rows_s[b * cuts + t : b * cuts + t + 1, :] = row[:, t * LANES : (t + 1) * LANES]

    last_tile = slots_deep - 8
    for lt in range(cuts):
        cut = slice(lt * LANES, (lt + 1) * LANES)
        pair_ref[lt, last_tile:, :] = jnp.full((8, LANES), EMPTY, I32)
        look_ref[lt, last_tile:, :] = jnp.zeros((8, LANES), I32)
        sign_ref[lt, last_tile:, :] = jnp.zeros((8, LANES), F32)
        look_ref[lt, 0:slots, :] = beta_ref[0, :, cut]
        pair_ref[lt, 0:slots, :] = beta_ref[1, :, cut]
        sign_ref[lt, 0:slots, :] = beta_ref[2, :, cut].astype(F32)

    blocks = [(lt, base) for base in range(0, pairs, LANES) for lt in range(cuts)]

    def invert(lt, base):
        size = min(LANES, -(-(pairs - base) // 8) * 8)
        ids = lax.broadcasted_iota(I32, (size, LANES), 0) + base

        def mark(e, acc):
            for k in range(9):
                acc = jnp.where(pair_ref[lt, pl.ds(9 * e + k, 1), :] == ids, 9 * e + k, acc)
            return acc

        acc = lax.fori_loop(0, slots // 9, mark, jnp.full((size, LANES), LANES - 1, I32))
        if size < LANES:
            acc = jnp.concatenate([acc, jnp.full((LANES - size, LANES), LANES - 1, I32)], axis=0)
        inv_ref[lt * LANES : (lt + 1) * LANES, base : base + LANES] = acc.T

    early = len(blocks) // 2
    for block in blocks[:early]:
        invert(*block)

    pl.semaphore_wait(barrier, parts - 1 + extra)

    def row_copy(j, slot):
        return pltpu.make_async_remote_copy(
            rows_s, table.at[slot], ts.at[j], tr.at[slot], device_id=(ga, j), device_id_type=MESH
        )

    each(lambda j: row_copy(j, me).start())

    right, left = lax.rem(ga + 1, groups), lax.rem(ga + groups - 1, groups)
    half_rows = rows_dev // 2

    def block_copy(src, dst, k, to):
        return pltpu.make_async_remote_copy(
            src, dst, xs.at[k], xr.at[k], device_id=(to, me), device_id_type=MESH
        )

    first_half, second_half = pl.ds(0, half_rows), pl.ds(half_rows, half_rows)
    hops = [
        block_copy(civ_ref, blk_ref.at[0], 0, right),
        block_copy(civ_ref, blk_ref.at[1], 1, left),
        block_copy(blk_ref.at[0, first_half], blk_ref.at[2, first_half], 2, right),
        block_copy(blk_ref.at[1, second_half], blk_ref.at[2, second_half], 3, left),
    ]
    if groups == 2:
        hops = hops[:1]
    for hop in hops[:2]:
        hop.start()
    table[me] = rows_s[...]

    for block in blocks[early:]:
        invert(*block)

    line_ref[...] = jnp.zeros_like(line_ref)
    line_ref[0:1, 0:pairs] = h_ref[...].reshape(1, pairs)
    strips = [jnp.broadcast_to(line_ref[0:1, k * LANES : (k + 1) * LANES], (8, LANES)) for k in range(3)]

    def h_of(index):
        low = jnp.bitwise_and(index, 127)
        high = lax.shift_right_logical(index, 7)
        out = jnp.zeros(index.shape, F32)
        for k in range(3):
            out = jnp.where(high == k, lanes_of(strips[k], low), out)
        return out

    def h_step(i, c):
        start = pl.multiple_of(8 * i, 8)
        for lt in range(cuts):
            hx_ref[lt, pl.ds(start, 8), :] = h_of(pair_ref[lt, pl.ds(start, 8), :])
        return c

    lax.fori_loop(0, slots_deep // 8, h_step, 0)

    s_row = packed_row(
        wide_ref, exc_ref[0, pl.ds(2 * ga, 1), :].astype(F32), exc_ref[0, pl.ds(2 * ga + 1, 1), :].astype(F32), slots,
        batch_ref[2 * ga].astype(F32), batch_ref[2 * ga + 1].astype(F32),
    )
    g_row = packed_row(
        wide_ref, exc_ref[2, pl.ds(2 * ga, 1), :].astype(F32), exc_ref[2, pl.ds(2 * ga + 1, 1), :].astype(F32), slots, 1.0, 1.0
    )
    p_row = packed_row(
        wide_ref, exc_ref[1, pl.ds(2 * ga, 1), :].astype(F32), exc_ref[1, pl.ds(2 * ga + 1, 1), :].astype(F32), slots,
        float(EMPTY), float(EMPTY),
    )
    wide_lane = lax.broadcasted_iota(I32, (1, 2 * LANES), 1)
    g_row = jnp.where(wide_lane < 2 * string, g_row, 0.0)
    h_row = jnp.concatenate(
        [h_of(jnp.broadcast_to(p_row[:, k : k + LANES], (8, LANES)).astype(I32))[0:1] for k in (0, LANES)], axis=1
    )
    meta = jnp.concatenate(
        [s_row, g_row, jnp.where(wide_lane < string, h_row, 0.0), jnp.where(wide_lane < string, 0.0, h_row),
         jnp.zeros((4, 2 * LANES), F32)], axis=0
    ).T[0:ROWS]
    source, sign = meta[:, 0:1], meta[:, 1:2]

    def choose(block, owner):
        ids = (lax.broadcasted_iota(I32, (ROWS, rows_dev), 1) + owner * rows_dev).astype(F32)
        pick = jnp.where(source == ids, sign, 0.0).astype(BF16)
        parts2 = split(block)
        return dot(pick, parts2[0], NN), dot(pick, parts2[1], NN)

    a_high, a_low = choose(civ_ref[...], ga)

    def arrive(j):
        for b in range(2):
            for t in range(cuts):
                line = table[j, b * cuts + t : b * cuts + t + 1, :]
                texp[b, cuts * j + t] = jnp.broadcast_to(line, (8, LANES))
                t_ref[b, pl.ds(cuts * j + t, 1), :] = line

    def finish_row(d, c):
        j = lax.rem(me + d, parts)
        row_copy(j, j).wait_recv()
        arrive(j)
        return c

    arrive(me)
    lax.fori_loop(1, parts, finish_row, 0)

    total_rows = parts * cuts
    chunk = 24
    halves = split(jnp.concatenate([t_ref[0], t_ref[1]], axis=0))
    full = jnp.concatenate(halves, axis=1)

    levels = 3 if total_rows % 64 == 0 else 0

    def mux(got, high, low_bit, count):
        for bit in range(low_bit, low_bit + count):
            n = got.shape[0] // 2
            got = got.reshape(n, 2, 8, LANES)
            mask = jnp.broadcast_to(jnp.bitwise_and(high, 1 << bit)[None], (n, 8, LANES)) != 0
            got = jnp.where(mask, got[:, 1], got[:, 0])
        return got

    sub = lax.broadcasted_iota(I32, (8, LANES), 0)
    tall = lax.broadcasted_iota(I32, (LANES, LANES), 0).astype(F32).astype(BF16)
    blank_hot, full_hot = jnp.zeros((LANES, LANES), BF16), jnp.ones((LANES, LANES), BF16)

    def match(lines):
        hot = []
        for low, _ in lines:
            line = jnp.broadcast_to(low, (16, LANES)).astype(F32).astype(BF16)
            hot.append(jnp.where(tall == jnp.concatenate([line] * 8, axis=0), full_hot, blank_hot))
        hot = jnp.concatenate(hot, axis=1) if len(hot) > 1 else hot[0]
        found = dot(full, jnp.concatenate([hot, hot], axis=0), NN)
        values = []
        for k, (_, high) in enumerate(lines):
            wide = jnp.broadcast_to(high, (8, LANES))
            near = jnp.bitwise_and(wide, 7) == sub
            block = lax.shift_right_logical(wide, 3 + levels)
            both = []
            for b in range(2):
                mine = found[b * total_rows : (b + 1) * total_rows, k * LANES : (k + 1) * LANES]
                mine = mux(mine.reshape(total_rows // 8, 8, LANES), wide, 3, levels)
                best = mine[0]
                for q in range(1, mine.shape[0]):
                    best = jnp.where(block == q, mine[q], best)
                both.append(jnp.sum(jnp.where(near, best, 0.0), axis=0, keepdims=True))
            values.append(both)
        return values

    def look_up(i, live):
        start = pl.multiple_of(8 * i, 8)
        low, high, acc = [], [], []
        for lt in range(cuts):
            src = look_ref[lt, pl.ds(start, 8), :]
            low.append(jnp.bitwise_and(src, 127))
            high.append(lax.shift_right_logical(src, 7))
            acc.append([jnp.zeros((8, LANES), F32)] * 2)
        direct = 1 if live == 8 else 0
        if direct:
            group = lax.shift_right_logical(high[0], 3)
            index = jnp.broadcast_to(low[0][None], (chunk, 8, LANES)).reshape(chunk * 8, LANES)
            for base in range(0, total_rows, chunk):
                for b in range(2):
                    got = texp[b, base : base + chunk].reshape(chunk * 8, LANES)
                    got = mux(lanes_of(got, index).reshape(chunk, 8, LANES), high[0], 0, 3)
                    for k in range(chunk // 8):
                        acc[0][b] = jnp.where(group == base // 8 + k, got[k], acc[0][b])
        spots = [(lt, r) for lt in range(direct, cuts) for r in range(live)]
        for n in range(0, len(spots), 2):
            some = spots[n : n + 2]
            values = match([(low[lt][r : r + 1], high[lt][r : r + 1]) for lt, r in some])
            for (lt, r), both in zip(some, values):
                for b in range(2):
                    acc[lt][b] = jnp.where(sub == r, both[b], acc[lt][b])
        for lt in range(cuts):
            factor = sign_ref[lt, pl.ds(start, 8), :]
            for b in range(2):
                vals_ref[b, lt, pl.ds(start, 8), :] = acc[lt][b] * factor

    def look_two(i, c):
        look_up(2 * i, 8)
        look_up(2 * i + 1, 8)
        return c

    tiles = slots_deep // 8
    relay = tiles // 4
    lax.fori_loop(0, relay, look_two, 0)
    for hop in hops[:2]:
        hop.wait_recv()
    for hop in hops[2:]:
        hop.start()
    lax.fori_loop(relay, tiles // 2, look_two, 0)
    for i in range(tiles // 2 * 2, tiles):
        look_up(i, min(8, slots - 8 * i))
    for hop in hops[2:]:
        hop.wait_recv()

    blank = jnp.zeros((LANES - slots_deep, LANES), F32)
    d2 = []
    for b in range(2):
        by_slot = jnp.concatenate(
            [jnp.concatenate([vals_ref[b, lt], blank], axis=0).T for lt in range(cuts)], axis=0
        )
        d2.append(split(jnp.concatenate(
            [lanes_of(by_slot, inv_ref[:, base : base + LANES]) for base in range(0, deep, LANES)], axis=1
        )))

    owners = [lax.rem(ga + groups - 1, groups), lax.rem(ga + 1, groups), lax.rem(ga + 2, groups)]
    for k in range(groups - 1):
        more = choose(blk_ref[k], owners[k])
        a_high, a_low = a_high + more[0], a_low + more[1]
    a2 = (a_high.astype(BF16), a_low.astype(BF16))
    a = a_high + a_low

    def times(left, right, dims):
        n = left[0].shape[0]
        both = dot(jnp.concatenate(left, axis=0), right[0], dims)
        return (both[:n] + both[n:]) + dot(left[0], right[1], dims)

    row = lax.broadcasted_iota(I32, (ROWS, 1), 0)
    first = row < string
    low_rows, high_rows = 96, 80
    m0 = times(tuple(p[:low_rows] for p in a2), d2[0], NN)
    m1 = times(tuple(p[high_rows:] for p in a2), d2[1], NN)
    m = jnp.where(
        first,
        jnp.concatenate([m0, jnp.zeros((ROWS - low_rows, deep), F32)], axis=0),
        jnp.concatenate([jnp.zeros((high_rows, deep), F32), m1], axis=0),
    )
    gram = times(a2, a2, NT)
    gram = jnp.concatenate([gram, jnp.zeros((ROWS, 2 * LANES - ROWS), F32)], axis=1)
    gram = jnp.where(first, gram, pltpu.roll(gram, 2 * LANES - string, 1))
    again = pltpu.roll(gram, string, 1)[:, 0:LANES]
    lane = lax.broadcasted_iota(I32, (ROWS, LANES), 1)
    gram = jnp.where(lane < string, gram[:, 0:LANES], again)
    local = jnp.where(first, row, row - string)
    folded = barrel(gram, lax.rem(SHIFT - local + 2 * LANES, LANES), 7)
    last = jnp.where(lane < SHIFT, m[:, 2 * LANES :], jnp.where(lane < SHIFT + HALF, folded, 0.0))
    for rg in range(ROWS // 8):
        for lt in range(3):
            k = rg * 3 + lt
            piece = last if lt == 2 else m[:, lt * LANES : (lt + 1) * LANES]
            tiles_ref[(k // per) % nc, k // per // nc, k % per] = piece[8 * rg : 8 * rg + 8]
    tiles_ref[nc - 1, parts // nc - 1, per - 1] = jnp.zeros((8, LANES), F32)

    def settled(count, sem):
        return pltpu.make_async_remote_copy(
            dummy.at[pl.ds(0, count)], dummy.at[pl.ds(0, count)], sem, sem, device_id=(right, me), device_id_type=MESH
        )

    chips = parts // nc
    chip = z * ny + y
    pair = pltpu.make_async_remote_copy(
        tiles_ref.at[1 - core], pair_buf, ps, pr, device_id=(ga, at(z, y, 1 - core)), device_id_type=MESH
    )
    pair.start()

    def drain_row(k, c):
        row_copy(far_first(k), me).wait_send()
        return c

    for b in range(2):
        from_a = jnp.sum(a * meta[:, 2 + b : 3 + b], axis=0, keepdims=True)
        for lt in range(cuts):
            cut = slice(lt * LANES, (lt + 1) * LANES)
            from_b = jnp.sum(vals_ref[b, lt] * hx_ref[lt], axis=0, keepdims=True)
            sigma_ref[b : b + 1, cut] = from_a[:, cut] + from_b
    pair.wait_recv()
    sums[...] = tiles_ref[core] + pair_buf[...]

    def part_copy(q):
        return pltpu.make_async_remote_copy(
            sums.at[q], got_ref.at[chip], ssem, rsem, device_id=(ga, q * nc + core), device_id_type=MESH
        )

    def send_part(k, c):
        part_copy(lax.rem(chip + 1 + lax.rem(k + (chips * 5) // 16, chips - 1), chips)).start()
        return c

    lax.fori_loop(0, chips - 1, send_part, 0)
    got_ref[chip] = sums[chip]
    lax.fori_loop(0, others, drain_row, 0)
    for hop in hops:
        hop.wait_send()
    pair.wait_send()
    settled((chips - 1) * per, rsem).wait_recv()
    zbuf[z] = jnp.sum(got_ref[...], axis=0)

    def z_copy(zz):
        return pltpu.make_async_remote_copy(
            zbuf.at[z], zbuf.at[z], zs, zr, device_id=(ga, at(zz, y, core)), device_id_type=MESH
        )

    for k in sorted(range(1, nz), key=lambda k: -min(k, nz - k)):
        z_copy(lax.rem(z + k, nz)).start()
    settled((chips - 1) * per, ssem).wait_send()
    if nz > 1:
        settled((nz - 1) * per, zr).wait_recv()

    ring = groups
    fx, fy = 1 - core, core

    def along(first, second):
        return (
            lax.rem(ga + first * fx + second * fy + 2 * ring, ring),
            lax.rem(y + first * fy + second * fx + 2 * ring, ring),
        )

    def piece(first, second, part):
        aa, yy = along(first, second)
        if part is None:
            return gat.at[aa, yy, core]
        return gat.at[aa, yy, core, pl.ds(part * (nz // 2), nz // 2)]

    def push(src, first, second, to_first, to_second, sem, part=None):
        aa, yy = along(to_first, to_second)
        return pltpu.make_async_remote_copy(
            src, piece(first, second, part), fs, fr.at[sem], device_id=(aa, at(z, yy, core)), device_id_type=MESH
        )

    def twin_copy(src, first, second):
        return pltpu.make_async_remote_copy(
            src, piece(first, second, None), cs, cr, device_id=(ga, at(z, y, 1 - core)), device_id_type=MESH
        )

    steps = [1] if ring == 2 else [-1, 1, 2]
    sides = [1] if ring == 2 else [-1, 1]
    row_of = [0] + steps

    def sem_of(f, kind):
        return f * 4 + kind

    def own_block(f):
        return zbuf if f == 0 else piece(row_of[f], 0, None)

    def send_second(f):
        for n, side in enumerate(sides):
            push(own_block(f), row_of[f], 0, 0, side, sem_of(f, n)).start()

    def await_first(n):
        push(zbuf, steps[n], 0, 0, 1, 16 + n).wait_recv()
        twin_copy(piece(steps[n], 0, None), steps[n], 0).start()
        send_second(n + 1)

    def await_second(f):
        for n, side in enumerate(sides):
            push(zbuf, row_of[f], -side, 0, side, sem_of(f, n)).wait_recv()
            if ring == 4:
                push(piece(row_of[f], -side, n), row_of[f], -side, 0, side, sem_of(f, 2 + n), n).start()
            twin_copy(piece(row_of[f], -side, None), row_of[f], -side).start()

    def await_halves(f):
        if ring == 4:
            for n in range(2):
                push(piece(row_of[f], 2, n), row_of[f], 2, 0, 1, sem_of(f, 2 + n), n).wait_recv()
            twin_copy(piece(row_of[f], 2, None), row_of[f], 2).start()

    for n in range(len(steps) - 1, -1, -1):
        back = steps[n] if ring == 2 else (steps[n] if steps[n] == 2 else -steps[n])
        push(zbuf, 0, 0, back, 0, 16 + n).start()
    send_second(0)
    twin_copy(zbuf, 0, 0).start()
    gat[ga, y, core] = zbuf[...]
    if ring == 2:
        await_first(0)
        await_second(0)
        await_second(1)
    else:
        await_first(0)
        await_first(1)
        await_second(0)
        await_first(2)
        await_second(1)
        await_second(2)
        await_halves(0)
        await_second(3)
        for f in (1, 2, 3):
            await_halves(f)
    sent = len(steps) * nz * per + len(row_of) * len(sides) * nz * per + (8 * (nz // 2) * per if ring == 4 else 0)
    if nz > 1:
        settled((nz - 1) * per, zs).wait_send()
    settled(sent, fs).wait_send()
    settled(planes * nz * per, cr).wait_recv()
    settled(planes * nz * per, cs).wait_send()


def place_kernel(groups, shape, slots, pairs, norm, exc_ref, gat, sigma_in, sigma_ref, density_ref, same_ref, mixed_ref,
                 r_ref, t_ref, wide_ref):
    nz, ny, nc = shape
    per = 64 // (nz * ny * nc)
    string = slots + 1
    deep = 3 * LANES
    sigma_ref[...] = sigma_in[...]
    row = lax.broadcasted_iota(I32, (ROWS, 1), 0)
    first = row < string
    local = jnp.where(first, row, row - string)
    amount = lax.rem(local - SHIFT + 2 * LANES, LANES)
    lane = lax.broadcasted_iota(I32, (ROWS, LANES), 1)
    weights = jnp.where((lane == SHIFT) | (lane == SHIFT + HALF - 1), 0.5, 1.0)
    weights = jnp.where((lane >= SHIFT) & (lane < SHIFT + HALF), weights, 0.0)
    strip = lax.broadcasted_iota(I32, (1, LANES), 1)
    wide = lax.broadcasted_iota(I32, (1, 2 * LANES), 1)
    span = -(-groups * ROWS // LANES) * LANES
    p_all = jnp.zeros((1, span), F32)
    exts = []
    for g in range(groups):
        rows = slice(g * ROWS, (g + 1) * ROWS)
        for rg in range(ROWS // 8):
            for lt in range(3):
                k = rg * 3 + lt
                j, s = k // per, k % per
                r_ref[g * ROWS + 8 * rg : g * ROWS + 8 * rg + 8, lt * LANES : (lt + 1) * LANES] = gat[
                    g, (j // nc) % ny, j % nc, j // (ny * nc), s
                ]
        ids = exc_ref[1, 2 * g : 2 * g + 2, :].astype(F32)
        p_row = packed_row(wide_ref.at[g], ids[0:1], ids[1:2], slots, float(pairs), float(pairs))
        p_row = jnp.where(wide < ROWS, p_row, 0.0)
        p_row = jnp.concatenate([p_row, jnp.zeros((1, span - 2 * LANES), F32)], axis=1)
        p_all = p_all + (pltpu.roll(p_row, g * ROWS, 1) if g else p_row)
        ends = []
        for b in range(2):
            line = wide_ref[g, b : b + 1, :]
            again = pltpu.roll(line, string, 1)
            line = jnp.where(strip < slots, line, jnp.where(strip == slots, float(pairs), again))
            ends.append(line)
        exts.append(jnp.concatenate(ends, axis=1))
    exts = jnp.concatenate(exts + [jnp.zeros((8 - groups, 2 * LANES), F32)], axis=0).T
    for g in range(groups):
        rows = slice(g * ROWS, (g + 1) * ROWS)
        half = barrel(r_ref[rows, 2 * LANES :] * weights, amount, 7)
        both = split(jnp.concatenate([jnp.where(first, half, 0.0), jnp.where(first, 0.0, half)], axis=1))
        right = (lax.broadcasted_iota(I32, (2 * LANES, deep), 1).astype(F32) == exts[:, g : g + 1]).astype(BF16)
        twice = dot(jnp.concatenate(both, axis=0), right, NN)
        t_ref[rows, :] = twice[:ROWS] + twice[ROWS:]
    tall = -(-(pairs + 1) // 8) * 8
    placing = (lax.broadcasted_iota(I32, (tall, groups * ROWS), 0).astype(F32) == p_all[:, : groups * ROWS]).astype(BF16)
    placed = dot2(placing, split(jnp.concatenate([r_ref[...], t_ref[...]], axis=1)), NN)
    mixed = placed[:, :deep]
    upper = jnp.concatenate([placed[:, deep:], jnp.zeros((deep - tall, deep), F32)], axis=0)
    root = math.sqrt(norm)
    same = upper + upper.T
    density_ref[0:1, :] = same[pairs : pairs + 1, 0:pairs] * (1.0 / root)
    density_ref[1:2, :] = mixed[pairs : pairs + 1, 0:pairs] * (1.0 / root)
    same_ref[...] = same[0:pairs, 0:pairs] * (1.0 / norm)
    mixed_ref[...] = mixed[0:pairs, 0:pairs] * (1.0 / root)


def body(shape, civec, batch_index, exc_alpha, exc_beta, one_body):
    vmem = pl.BlockSpec(memory_space=pltpu.VMEM)
    smem = pl.BlockSpec(memory_space=pltpu.SMEM)
    anywhere = pl.BlockSpec(memory_space=pl.ANY)
    nz, ny, nc = shape
    parts = nz * ny * nc
    per = 64 // parts
    groups = lax.axis_size("alpha")
    rows_dev, width = civec.shape
    total = batch_index.shape[0]
    batch = total // groups
    slots = exc_alpha.shape[2]
    pairs = one_body.shape[0]
    deep = 3 * LANES
    cuts = width // LANES
    slots_deep = -(-slots // 8) * 8
    dma = pltpu.SemaphoreType.DMA
    sigma, gat = pl.pallas_call(
        functools.partial(main_kernel, groups, shape, slots, pairs),
        out_shape=(
            jax.ShapeDtypeStruct((batch, width), F32),
            jax.ShapeDtypeStruct((groups, ny, nc, nz, per, 8, LANES), F32),
        ),
        in_specs=[smem, vmem, anywhere, vmem, anywhere],
        out_specs=(vmem, vmem),
        scratch_shapes=[
            pltpu.VMEM((3, slots, width), I32),
            pltpu.VMEM((rows_dev, width), F32),
            pltpu.VMEM((cuts, slots_deep, LANES), I32),
            pltpu.VMEM((cuts, slots_deep, LANES), I32),
            pltpu.VMEM((cuts, slots_deep, LANES), F32),
            pltpu.VMEM((cuts, slots_deep, LANES), F32),
            pltpu.VMEM((width, deep), I32),
            pltpu.VMEM((2 * cuts, LANES), F32),
            pltpu.VMEM((parts, 2 * cuts, LANES), F32),
            pltpu.VMEM((2, parts * cuts, 8, LANES), F32),
            pltpu.VMEM((2, parts * cuts, LANES), F32),
            pltpu.VMEM((2, cuts, slots_deep, LANES), F32),
            pltpu.VMEM((max(groups - 1, 2), rows_dev, width), F32),
            pltpu.VMEM((8, deep), F32),
            pltpu.VMEM((8, LANES), F32),
            pltpu.VMEM((nc, parts // nc, per, 8, LANES), F32),
            pltpu.VMEM((parts // nc, per, 8, LANES), F32),
            pltpu.VMEM((parts // nc, per, 8, LANES), F32),
            pltpu.VMEM((parts // nc, per, 8, LANES), F32),
            pltpu.VMEM((nz, per, 8, LANES), F32),
            pltpu.VMEM((groups * ny * nz * per, 8, LANES), F32),
            dma((2,)),
            dma((parts,)), dma((parts,)),
            dma((4,)), dma((4,)),
            dma, dma, dma, dma, dma, dma, dma,
            dma((20,)),
            dma, dma,
        ],
        compiler_params=pltpu.CompilerParams(collective_id=0, has_side_effects=True),
        name="main",
    )(batch_index, exc_alpha, exc_beta.swapaxes(1, 2), one_body, civec)
    return tuple(pl.pallas_call(
        functools.partial(place_kernel, groups, shape, slots, pairs, total * width * parts),
        out_shape=(
            jax.ShapeDtypeStruct((batch, width), F32),
            jax.ShapeDtypeStruct((2, pairs), F32),
            jax.ShapeDtypeStruct((pairs, pairs), F32),
            jax.ShapeDtypeStruct((pairs, pairs), F32),
        ),
        in_specs=[vmem, vmem, vmem],
        out_specs=(vmem, vmem, vmem, vmem),
        scratch_shapes=[pltpu.VMEM((groups * ROWS, deep), F32)] * 2 + [pltpu.VMEM((groups, 8, LANES), F32)],
        name="place",
    )(exc_alpha, gat, sigma))


def solution(mesh, shape=(8, 4, 2)):
    in_specs = (P("alpha", "beta"), P(), P(), P(None, "beta", None), P())
    out_specs = (P("alpha", "beta"), P(), P(), P())
    return jax.shard_map(
        functools.partial(body, shape), mesh=mesh, in_specs=in_specs, out_specs=out_specs, check_vma=False
    )
```

```python
import functools
import math

import jax
import jax.numpy as jnp
from jax import lax
from jax.experimental import pallas as pl
from jax.experimental.pallas import tpu as pltpu
from jax.sharding import PartitionSpec as P

MESH = pl.DeviceIdType.MESH
F32, BF16, I32 = jnp.float32, jnp.bfloat16, jnp.int32
LANES = 128
HALF = 42
SHIFT = 68
ROWS = 168
EMPTY = 511
NT = (((1,), (1,)), ((), ()))
NN = (((1,), (0,)), ((), ()))
ALONG = lax.GatherDimensionNumbers(
    offset_dims=(), collapsed_slice_dims=(1,), start_index_map=(1,), operand_batching_dims=(0,), start_indices_batching_dims=(0,)
)


def split(x):
    high = x.astype(BF16)
    return high, (x - high.astype(F32)).astype(BF16)


def dot(a, b, dims):
    return lax.dot_general(a, b, dims, preferred_element_type=F32)


def dot3(a, b, dims):
    return dot(a[0], b[0], dims) + (dot(a[0], b[1], dims) + dot(a[1], b[0], dims))


def dot2(a, b, dims):
    return dot(a, b[0], dims) + dot(a, b[1], dims)


def lanes_of(x, index):
    return lax.gather(x, index[..., None], ALONG, (1, 1), mode=lax.GatherScatterMode.PROMISE_IN_BOUNDS)


def barrel(x, amount, bits):
    for bit in range(bits):
        moved = pltpu.roll(x, 1 << bit, 1)
        x = jnp.where(lax.rem(lax.div(amount, 1 << bit), 2) == 1, moved, x)
    return x


def packed_row(wide_ref, first, second, slots, end_first, end_second):
    string = slots + 1
    wide_ref[...] = jnp.zeros_like(wide_ref)
    wide_ref[0:1, 0:slots] = first
    wide_ref[1:2, 0:slots] = second
    lane = lax.broadcasted_iota(I32, (1, 2 * LANES), 1)
    blank = jnp.zeros((1, LANES), F32)
    one = jnp.concatenate([wide_ref[0:1, :], blank], axis=1)
    two = pltpu.roll(jnp.concatenate([wide_ref[1:2, :], blank], axis=1), string, 1)
    out = jnp.where(lane < string, one, two)
    out = jnp.where(lane == slots, end_first, jnp.where(lane == string + slots, end_second, out))
    return jnp.where(lane < 2 * string, out, float(EMPTY))


def main_kernel(groups, shape, slots, pairs, batch_ref, exc_ref, beta_hbm, h_ref, civ_hbm, sigma_ref, gat,
                beta_ref, civ_ref, pair_ref, look_ref, sign_ref, hx_ref, inv_ref, rows_s, table, texp, t_ref, vals_ref, blk_ref, line_ref,
                wide_ref, tiles_ref, pair_buf, sums, y_got, y_sum, got_ref, zbuf, dummy,
                in_sem, ts, tr, ys, yr, ws, wr, vs, vr, xs, xr, ps, pr, ssem, rsem, zs, zr, fs, fr, cs, cr):
    nz, ny, nc = shape
    parts = nz * ny * nc
    per = 64 // parts
    width = beta_ref.shape[2]
    cuts = width // LANES
    deep = 3 * LANES
    slots_deep = look_ref.shape[1]
    rows_dev = civ_ref.shape[0]
    string = slots + 1
    ga = lax.axis_index("alpha")
    me = lax.axis_index("beta")
    z, y, core = me // (ny * nc), (me // nc) % ny, me % nc
    planes = groups * ny

    def at(zz, yy, cc):
        return (zz * ny + yy) * nc + cc

    loads = [pltpu.make_async_copy(civ_hbm, civ_ref, in_sem.at[0]), pltpu.make_async_copy(beta_hbm, beta_ref, in_sem.at[1])]
    for load in loads:
        load.start()
    barrier = pltpu.get_barrier_semaphore()
    twin = at(z, y, 1 - core)
    z_far = sorted(range(1, nz), key=lambda k: -min(k, nz - k))
    y_far = sorted(range(1, ny), key=lambda k: -min(k, ny - k))
    for k in z_far:
        pl.semaphore_signal(barrier, inc=1, device_id=(ga, at(lax.rem(z + k, nz), y, core)), device_id_type=MESH)

    def spread_of(k):
        return min(k // ny, groups - k // ny) + min(k % ny, ny - k % ny)

    near = sorted(range(1, planes), key=spread_of)
    around = [(lax.rem(ga + k // ny, groups), lax.rem(y + k % ny, ny), k // ny) for k in near]
    for aa, yy, _ in around[::-1]:
        pl.semaphore_signal(barrier, inc=1, device_id=(aa, at(z, yy, core)), device_id_type=MESH)
    pl.semaphore_signal(barrier, inc=1, device_id=(ga, twin), device_id_type=MESH)
    for load in loads:
        load.wait()
    for b in range(2):
        row = civ_ref[pl.ds(lax.rem(batch_ref[2 * ga + b], rows_dev), 1), :]
        for t in range(cuts):
            rows_s[b * cuts + t : b * cuts + t + 1, :] = row[:, t * LANES : (t + 1) * LANES]

    last_tile = slots_deep - 8
    for lt in range(cuts):
        cut = slice(lt * LANES, (lt + 1) * LANES)
        pair_ref[lt, last_tile:, :] = jnp.full((8, LANES), EMPTY, I32)
        look_ref[lt, last_tile:, :] = jnp.zeros((8, LANES), I32)
        sign_ref[lt, last_tile:, :] = jnp.zeros((8, LANES), F32)
        look_ref[lt, 0:slots, :] = beta_ref[0, :, cut]
        pair_ref[lt, 0:slots, :] = beta_ref[1, :, cut]
        sign_ref[lt, 0:slots, :] = beta_ref[2, :, cut].astype(F32)

    blocks = [(lt, base) for base in range(0, pairs, LANES) for lt in range(cuts)]

    def invert(lt, base):
        size = min(LANES, -(-(pairs - base) // 8) * 8)
        ids = lax.broadcasted_iota(I32, (size, LANES), 0) + base

        def mark(e, acc):
            for k in range(9):
                acc = jnp.where(pair_ref[lt, pl.ds(9 * e + k, 1), :] == ids, 9 * e + k, acc)
            return acc

        acc = lax.fori_loop(0, slots // 9, mark, jnp.full((size, LANES), LANES - 1, I32))
        if size < LANES:
            acc = jnp.concatenate([acc, jnp.full((LANES - size, LANES), LANES - 1, I32)], axis=0)
        inv_ref[lt * LANES : (lt + 1) * LANES, base : base + LANES] = acc.T

    early = 2
    for block in blocks[:early]:
        invert(*block)

    pl.semaphore_wait(barrier, nz - 1 + planes - 1 + 1)

    def row_copy(to_z, slot_z):
        return pltpu.make_async_remote_copy(
            rows_s, table.at[y, core, slot_z], ts.at[to_z], tr.at[slot_z],
            device_id=(ga, at(to_z, y, core)), device_id_type=MESH,
        )

    def line_copy(to_y, slot_y):
        return pltpu.make_async_remote_copy(
            table.at[y, core], table.at[slot_y, core], ys.at[to_y], yr.at[slot_y],
            device_id=(ga, at(z, to_y, core)), device_id_type=MESH,
        )

    def twin_line(slot_y, slot_c):
        return pltpu.make_async_remote_copy(
            table.at[slot_y, core], table.at[slot_y, slot_c], ws.at[slot_y], wr.at[slot_y],
            device_id=(ga, twin), device_id_type=MESH,
        )

    for k in z_far:
        row_copy(lax.rem(z + k, nz), z).start()

    right, left = lax.rem(ga + 1, groups), lax.rem(ga + groups - 1, groups)
    half_rows = rows_dev // 2

    def block_copy(src, dst, k, to):
        return pltpu.make_async_remote_copy(
            src, dst, xs.at[k], xr.at[k], device_id=(to, me), device_id_type=MESH
        )

    first_half, second_half = pl.ds(0, half_rows), pl.ds(half_rows, half_rows)
    hops = [
        block_copy(civ_ref, blk_ref.at[0], 0, right),
        block_copy(civ_ref, blk_ref.at[1], 1, left),
        block_copy(blk_ref.at[0, first_half], blk_ref.at[2, first_half], 2, right),
        block_copy(blk_ref.at[1, second_half], blk_ref.at[2, second_half], 3, left),
    ]
    if groups == 2:
        hops = hops[:1]
    for hop in hops[:2]:
        hop.start()
    table[y, core, z] = rows_s[...]

    for block in blocks[early:]:
        invert(*block)

    line_ref[...] = jnp.zeros_like(line_ref)
    line_ref[0:1, 0:pairs] = h_ref[...].reshape(1, pairs)
    strips = [jnp.broadcast_to(line_ref[0:1, k * LANES : (k + 1) * LANES], (8, LANES)) for k in range(3)]

    def h_of(index):
        low = jnp.bitwise_and(index, 127)
        high = lax.shift_right_logical(index, 7)
        out = jnp.zeros(index.shape, F32)
        for k in range(3):
            out = jnp.where(high == k, lanes_of(strips[k], low), out)
        return out

    def h_step(i, c):
        start = pl.multiple_of(8 * i, 8)
        for lt in range(cuts):
            hx_ref[lt, pl.ds(start, 8), :] = h_of(pair_ref[lt, pl.ds(start, 8), :])
        return c

    lax.fori_loop(0, slots_deep // 8, h_step, 0)

    s_row = packed_row(
        wide_ref, exc_ref[0, pl.ds(2 * ga, 1), :].astype(F32), exc_ref[0, pl.ds(2 * ga + 1, 1), :].astype(F32), slots,
        batch_ref[2 * ga].astype(F32), batch_ref[2 * ga + 1].astype(F32),
    )
    g_row = packed_row(
        wide_ref, exc_ref[2, pl.ds(2 * ga, 1), :].astype(F32), exc_ref[2, pl.ds(2 * ga + 1, 1), :].astype(F32), slots, 1.0, 1.0
    )
    p_row = packed_row(
        wide_ref, exc_ref[1, pl.ds(2 * ga, 1), :].astype(F32), exc_ref[1, pl.ds(2 * ga + 1, 1), :].astype(F32), slots,
        float(EMPTY), float(EMPTY),
    )
    wide_lane = lax.broadcasted_iota(I32, (1, 2 * LANES), 1)
    g_row = jnp.where(wide_lane < 2 * string, g_row, 0.0)
    h_row = jnp.concatenate(
        [h_of(jnp.broadcast_to(p_row[:, k : k + LANES], (8, LANES)).astype(I32))[0:1] for k in (0, LANES)], axis=1
    )
    meta = jnp.concatenate(
        [s_row, g_row, jnp.where(wide_lane < string, h_row, 0.0), jnp.where(wide_lane < string, 0.0, h_row),
         jnp.zeros((4, 2 * LANES), F32)], axis=0
    ).T[0:ROWS]
    source, sign = meta[:, 0:1], meta[:, 1:2]

    def choose(block, owner):
        ids = (lax.broadcasted_iota(I32, (ROWS, rows_dev), 1) + owner * rows_dev).astype(F32)
        pick = jnp.where(source == ids, sign, 0.0).astype(BF16)
        parts2 = split(block)
        return dot(pick, parts2[0], NN), dot(pick, parts2[1], NN)

    a_high, a_low = choose(civ_ref[...], ga)

    def arrive(yy, cc):
        def step(zz, c):
            for b in range(2):
                for t in range(cuts):
                    line = table[yy, cc, zz, b * cuts + t : b * cuts + t + 1, :]
                    spot = cuts * at(zz, yy, cc) + t
                    texp[b, spot] = jnp.broadcast_to(line, (8, LANES))
                    t_ref[b, pl.ds(spot, 1), :] = line
            return c

        lax.fori_loop(0, nz, step, 0)

    for k in z_far[::-1]:
        zz = lax.rem(z + k, nz)
        row_copy(zz, zz).wait_recv()
    for k in y_far:
        line_copy(lax.rem(y + k, ny), y).start()
    twin_line(y, core).start()
    arrive(y, core)
    for k in y_far[::-1]:
        yy = lax.rem(y + k, ny)
        line_copy(yy, yy).wait_recv()
        twin_line(yy, core).start()
        arrive(yy, core)
    for k in [0] + y_far[::-1]:
        yy = lax.rem(y + k, ny)
        twin_line(yy, 1 - core).wait_recv()
        arrive(yy, 1 - core)

    total_rows = parts * cuts
    chunk = 24
    halves = split(jnp.concatenate([t_ref[0], t_ref[1]], axis=0))
    full = jnp.concatenate(halves, axis=1)

    levels = 3 if total_rows % 64 == 0 else 0

    def mux(got, high, low_bit, count):
        for bit in range(low_bit, low_bit + count):
            n = got.shape[0] // 2
            got = got.reshape(n, 2, 8, LANES)
            mask = jnp.broadcast_to(jnp.bitwise_and(high, 1 << bit)[None], (n, 8, LANES)) != 0
            got = jnp.where(mask, got[:, 1], got[:, 0])
        return got

    sub = lax.broadcasted_iota(I32, (8, LANES), 0)
    tall = lax.broadcasted_iota(I32, (LANES, LANES), 0).astype(F32).astype(BF16)
    blank_hot, full_hot = jnp.zeros((LANES, LANES), BF16), jnp.ones((LANES, LANES), BF16)

    def match(lines):
        hot = []
        for low, _ in lines:
            line = jnp.broadcast_to(low, (16, LANES)).astype(F32).astype(BF16)
            hot.append(jnp.where(tall == jnp.concatenate([line] * 8, axis=0), full_hot, blank_hot))
        hot = jnp.concatenate(hot, axis=1) if len(hot) > 1 else hot[0]
        found = dot(full, jnp.concatenate([hot, hot], axis=0), NN)
        values = []
        for k, (_, high) in enumerate(lines):
            wide = jnp.broadcast_to(high, (8, LANES))
            near = jnp.bitwise_and(wide, 7) == sub
            block = lax.shift_right_logical(wide, 3 + levels)
            both = []
            for b in range(2):
                mine = found[b * total_rows : (b + 1) * total_rows, k * LANES : (k + 1) * LANES]
                mine = mux(mine.reshape(total_rows // 8, 8, LANES), wide, 3, levels)
                best = mine[0]
                for q in range(1, mine.shape[0]):
                    best = jnp.where(block == q, mine[q], best)
                both.append(jnp.sum(jnp.where(near, best, 0.0), axis=0, keepdims=True))
            values.append(both)
        return values

    def look_up(i, live):
        start = pl.multiple_of(8 * i, 8)
        low, high, acc = [], [], []
        for lt in range(cuts):
            src = look_ref[lt, pl.ds(start, 8), :]
            low.append(jnp.bitwise_and(src, 127))
            high.append(lax.shift_right_logical(src, 7))
            acc.append([jnp.zeros((8, LANES), F32)] * 2)
        direct = 1 if live == 8 else 0
        if direct:
            group = lax.shift_right_logical(high[0], 3)
            index = jnp.broadcast_to(low[0][None], (chunk, 8, LANES)).reshape(chunk * 8, LANES)
            for base in range(0, total_rows, chunk):
                for b in range(2):
                    got = texp[b, base : base + chunk].reshape(chunk * 8, LANES)
                    got = mux(lanes_of(got, index).reshape(chunk, 8, LANES), high[0], 0, 3)
                    for k in range(chunk // 8):
                        acc[0][b] = jnp.where(group == base // 8 + k, got[k], acc[0][b])
        spots = [(lt, r) for lt in range(direct, cuts) for r in range(live)]
        for n in range(0, len(spots), 2):
            some = spots[n : n + 2]
            values = match([(low[lt][r : r + 1], high[lt][r : r + 1]) for lt, r in some])
            for (lt, r), both in zip(some, values):
                for b in range(2):
                    acc[lt][b] = jnp.where(sub == r, both[b], acc[lt][b])
        for lt in range(cuts):
            factor = sign_ref[lt, pl.ds(start, 8), :]
            for b in range(2):
                vals_ref[b, lt, pl.ds(start, 8), :] = acc[lt][b] * factor

    def look_two(i, c):
        look_up(2 * i, 8)
        look_up(2 * i + 1, 8)
        return c

    tiles = slots_deep // 8
    relay = tiles // 4
    lax.fori_loop(0, relay, look_two, 0)
    for hop in hops[:2]:
        hop.wait_recv()
    for hop in hops[2:]:
        hop.start()
    lax.fori_loop(relay, tiles // 2, look_two, 0)
    for i in range(tiles // 2 * 2, tiles):
        look_up(i, min(8, slots - 8 * i))
    for hop in hops[2:]:
        hop.wait_recv()

    blank = jnp.zeros((LANES - slots_deep, LANES), F32)
    d2 = []
    for b in range(2):
        by_slot = jnp.concatenate(
            [jnp.concatenate([vals_ref[b, lt], blank], axis=0).T for lt in range(cuts)], axis=0
        )
        d2.append(split(jnp.concatenate(
            [lanes_of(by_slot, inv_ref[:, base : base + LANES]) for base in range(0, deep, LANES)], axis=1
        )))

    owners = [lax.rem(ga + groups - 1, groups), lax.rem(ga + 1, groups), lax.rem(ga + 2, groups)]
    for k in range(groups - 1):
        more = choose(blk_ref[k], owners[k])
        a_high, a_low = a_high + more[0], a_low + more[1]
    a2 = (a_high.astype(BF16), a_low.astype(BF16))
    a = a_high + a_low

    def times(left, right, dims):
        n = left[0].shape[0]
        both = dot(jnp.concatenate(left, axis=0), right[0], dims)
        return (both[:n] + both[n:]) + dot(left[0], right[1], dims)

    row = lax.broadcasted_iota(I32, (ROWS, 1), 0)
    first = row < string
    low_rows, high_rows = 96, 80
    m0 = times(tuple(p[:low_rows] for p in a2), d2[0], NN)
    m1 = times(tuple(p[high_rows:] for p in a2), d2[1], NN)
    m = jnp.where(
        first,
        jnp.concatenate([m0, jnp.zeros((ROWS - low_rows, deep), F32)], axis=0),
        jnp.concatenate([jnp.zeros((high_rows, deep), F32), m1], axis=0),
    )
    gram = times(a2, a2, NT)
    gram = jnp.concatenate([gram, jnp.zeros((ROWS, 2 * LANES - ROWS), F32)], axis=1)
    gram = jnp.where(first, gram, pltpu.roll(gram, 2 * LANES - string, 1))
    again = pltpu.roll(gram, string, 1)[:, 0:LANES]
    lane = lax.broadcasted_iota(I32, (ROWS, LANES), 1)
    gram = jnp.where(lane < string, gram[:, 0:LANES], again)
    local = jnp.where(first, row, row - string)
    folded = barrel(gram, lax.rem(SHIFT - local + 2 * LANES, LANES), 7)
    last = jnp.where(lane < SHIFT, m[:, 2 * LANES :], jnp.where(lane < SHIFT + HALF, folded, 0.0))
    for rg in range(ROWS // 8):
        for lt in range(3):
            k = rg * 3 + lt
            piece = last if lt == 2 else m[:, lt * LANES : (lt + 1) * LANES]
            tiles_ref[(k // per) % nc, k // per // nc, k % per] = piece[8 * rg : 8 * rg + 8]
    tiles_ref[nc - 1, parts // nc - 1, per - 1] = jnp.zeros((8, LANES), F32)

    def settled(count, sem):
        return pltpu.make_async_remote_copy(
            dummy.at[pl.ds(0, count)], dummy.at[pl.ds(0, count)], sem, sem, device_id=(right, me), device_id_type=MESH
        )

    chips = parts // nc
    chip = z * ny + y
    pair = pltpu.make_async_remote_copy(
        tiles_ref.at[1 - core], pair_buf, ps, pr, device_id=(ga, twin), device_id_type=MESH
    )
    pair.start()

    for b in range(2):
        from_a = jnp.sum(a * meta[:, 2 + b : 3 + b], axis=0, keepdims=True)
        for lt in range(cuts):
            cut = slice(lt * LANES, (lt + 1) * LANES)
            from_b = jnp.sum(vals_ref[b, lt] * hx_ref[lt], axis=0, keepdims=True)
            sigma_ref[b : b + 1, cut] = from_a[:, cut] + from_b
    pair.wait_recv()
    sums[...] = tiles_ref[core] + pair_buf[...]

    def y_part(yy):
        return pltpu.make_async_remote_copy(
            sums.at[pl.ds(yy * nz, nz)], y_got.at[y], ssem, rsem, device_id=(ga, at(z, yy, core)), device_id_type=MESH
        )

    for k in y_far:
        y_part(lax.rem(y + k, ny)).start()
    y_got[y] = sums[pl.ds(y * nz, nz)]
    for k in z_far:
        row_copy(lax.rem(z + k, nz), z).wait_send()
    for k in y_far:
        line_copy(lax.rem(y + k, ny), y).wait_send()
    for yy in range(ny):
        twin_line(yy, core).wait_send()
    for hop in hops:
        hop.wait_send()
    pair.wait_send()
    if ny > 1:
        settled((ny - 1) * nz * per, rsem).wait_recv()
    y_sum[...] = jnp.sum(y_got[...], axis=0)

    def z_part(zz):
        return pltpu.make_async_remote_copy(
            y_sum.at[zz], got_ref.at[z], vs, vr, device_id=(ga, at(zz, y, core)), device_id_type=MESH
        )

    for k in z_far:
        z_part(lax.rem(z + k, nz)).start()
    got_ref[z] = y_sum[z]
    if ny > 1:
        settled((ny - 1) * nz * per, ssem).wait_send()
    if nz > 1:
        settled((nz - 1) * per, vr).wait_recv()
    zbuf[z] = jnp.sum(got_ref[...], axis=0)

    def z_copy(zz):
        return pltpu.make_async_remote_copy(
            zbuf.at[z], zbuf.at[z], zs, zr, device_id=(ga, at(zz, y, core)), device_id_type=MESH
        )

    for k in sorted(range(1, nz), key=lambda k: -min(k, nz - k)):
        z_copy(lax.rem(z + k, nz)).start()
    if nz > 1:
        settled((nz - 1) * per, vs).wait_send()
    if nz > 1:
        settled((nz - 1) * per, zr).wait_recv()

    def plane_copy(src, aa, yy, slot_a, slot_y):
        return pltpu.make_async_remote_copy(
            src, gat.at[slot_a, slot_y, core], fs, fr.at[slot_a, slot_y],
            device_id=(aa, at(z, yy, core)), device_id_type=MESH,
        )

    def twin_copy(src, slot_a, slot_y):
        return pltpu.make_async_remote_copy(
            src, gat.at[slot_a, slot_y, core], cs, cr,
            device_id=(ga, at(z, y, 1 - core)), device_id_type=MESH,
        )

    for aa, yy, _ in around[::-1]:
        plane_copy(zbuf, aa, yy, ga, y).start()
    twin_copy(zbuf, ga, y).start()
    gat[ga, y, core] = zbuf[...]
    for aa, yy, _ in around:
        plane_copy(zbuf, aa, yy, aa, yy).wait_recv()
        twin_copy(gat.at[aa, yy, core], aa, yy).start()
    if nz > 1:
        settled((nz - 1) * per, zs).wait_send()
    settled((planes - 1) * nz * per, fs).wait_send()
    settled(planes * nz * per, cr).wait_recv()
    settled(planes * nz * per, cs).wait_send()


def place_kernel(groups, shape, slots, pairs, norm, exc_ref, gat, sigma_in, sigma_ref, density_ref, same_ref, mixed_ref,
                 r_ref, t_ref, wide_ref):
    nz, ny, nc = shape
    per = 64 // (nz * ny * nc)
    string = slots + 1
    deep = 3 * LANES
    sigma_ref[...] = sigma_in[...]
    row = lax.broadcasted_iota(I32, (ROWS, 1), 0)
    first = row < string
    local = jnp.where(first, row, row - string)
    amount = lax.rem(local - SHIFT + 2 * LANES, LANES)
    lane = lax.broadcasted_iota(I32, (ROWS, LANES), 1)
    weights = jnp.where((lane == SHIFT) | (lane == SHIFT + HALF - 1), 0.5, 1.0)
    weights = jnp.where((lane >= SHIFT) & (lane < SHIFT + HALF), weights, 0.0)
    strip = lax.broadcasted_iota(I32, (1, LANES), 1)
    wide = lax.broadcasted_iota(I32, (1, 2 * LANES), 1)
    span = -(-groups * ROWS // LANES) * LANES
    p_all = jnp.zeros((1, span), F32)
    exts = []
    for g in range(groups):
        rows = slice(g * ROWS, (g + 1) * ROWS)
        for rg in range(ROWS // 8):
            for lt in range(3):
                k = rg * 3 + lt
                j, s = k // per, k % per
                r_ref[g * ROWS + 8 * rg : g * ROWS + 8 * rg + 8, lt * LANES : (lt + 1) * LANES] = gat[
                    g, j // nc // nz, j % nc, (j // nc) % nz, s
                ]
        ids = exc_ref[1, 2 * g : 2 * g + 2, :].astype(F32)
        p_row = packed_row(wide_ref.at[g], ids[0:1], ids[1:2], slots, float(pairs), float(pairs))
        p_row = jnp.where(wide < ROWS, p_row, 0.0)
        p_row = jnp.concatenate([p_row, jnp.zeros((1, span - 2 * LANES), F32)], axis=1)
        p_all = p_all + (pltpu.roll(p_row, g * ROWS, 1) if g else p_row)
        ends = []
        for b in range(2):
            line = wide_ref[g, b : b + 1, :]
            again = pltpu.roll(line, string, 1)
            line = jnp.where(strip < slots, line, jnp.where(strip == slots, float(pairs), again))
            ends.append(line)
        exts.append(jnp.concatenate(ends, axis=1))
    exts = jnp.concatenate(exts + [jnp.zeros((8 - groups, 2 * LANES), F32)], axis=0).T
    for g in range(groups):
        rows = slice(g * ROWS, (g + 1) * ROWS)
        half = barrel(r_ref[rows, 2 * LANES :] * weights, amount, 7)
        both = split(jnp.concatenate([jnp.where(first, half, 0.0), jnp.where(first, 0.0, half)], axis=1))
        right = (lax.broadcasted_iota(I32, (2 * LANES, deep), 1).astype(F32) == exts[:, g : g + 1]).astype(BF16)
        twice = dot(jnp.concatenate(both, axis=0), right, NN)
        t_ref[rows, :] = twice[:ROWS] + twice[ROWS:]
    tall = -(-(pairs + 1) // 8) * 8
    placing = (lax.broadcasted_iota(I32, (tall, groups * ROWS), 0).astype(F32) == p_all[:, : groups * ROWS]).astype(BF16)
    placed = dot2(placing, split(jnp.concatenate([r_ref[...], t_ref[...]], axis=1)), NN)
    mixed = placed[:, :deep]
    upper = jnp.concatenate([placed[:, deep:], jnp.zeros((deep - tall, deep), F32)], axis=0)
    root = math.sqrt(norm)
    same = upper + upper.T
    density_ref[0:1, :] = same[pairs : pairs + 1, 0:pairs] * (1.0 / root)
    density_ref[1:2, :] = mixed[pairs : pairs + 1, 0:pairs] * (1.0 / root)
    same_ref[...] = same[0:pairs, 0:pairs] * (1.0 / norm)
    mixed_ref[...] = mixed[0:pairs, 0:pairs] * (1.0 / root)


def body(shape, civec, batch_index, exc_alpha, exc_beta, one_body):
    vmem = pl.BlockSpec(memory_space=pltpu.VMEM)
    smem = pl.BlockSpec(memory_space=pltpu.SMEM)
    anywhere = pl.BlockSpec(memory_space=pl.ANY)
    nz, ny, nc = shape
    parts = nz * ny * nc
    per = 64 // parts
    groups = lax.axis_size("alpha")
    rows_dev, width = civec.shape
    total = batch_index.shape[0]
    batch = total // groups
    slots = exc_alpha.shape[2]
    pairs = one_body.shape[0]
    deep = 3 * LANES
    cuts = width // LANES
    slots_deep = -(-slots // 8) * 8
    dma = pltpu.SemaphoreType.DMA
    sigma, gat = pl.pallas_call(
        functools.partial(main_kernel, groups, shape, slots, pairs),
        out_shape=(
            jax.ShapeDtypeStruct((batch, width), F32),
            jax.ShapeDtypeStruct((groups, ny, nc, nz, per, 8, LANES), F32),
        ),
        in_specs=[smem, vmem, anywhere, vmem, anywhere],
        out_specs=(vmem, vmem),
        scratch_shapes=[
            pltpu.VMEM((3, slots, width), I32),
            pltpu.VMEM((rows_dev, width), F32),
            pltpu.VMEM((cuts, slots_deep, LANES), I32),
            pltpu.VMEM((cuts, slots_deep, LANES), I32),
            pltpu.VMEM((cuts, slots_deep, LANES), F32),
            pltpu.VMEM((cuts, slots_deep, LANES), F32),
            pltpu.VMEM((width, deep), I32),
            pltpu.VMEM((2 * cuts, LANES), F32),
            pltpu.VMEM((ny, nc, nz, 2 * cuts, LANES), F32),
            pltpu.VMEM((2, parts * cuts, 8, LANES), F32),
            pltpu.VMEM((2, parts * cuts, LANES), F32),
            pltpu.VMEM((2, cuts, slots_deep, LANES), F32),
            pltpu.VMEM((max(groups - 1, 2), rows_dev, width), F32),
            pltpu.VMEM((8, deep), F32),
            pltpu.VMEM((8, LANES), F32),
            pltpu.VMEM((nc, parts // nc, per, 8, LANES), F32),
            pltpu.VMEM((parts // nc, per, 8, LANES), F32),
            pltpu.VMEM((parts // nc, per, 8, LANES), F32),
            pltpu.VMEM((ny, nz, per, 8, LANES), F32),
            pltpu.VMEM((nz, per, 8, LANES), F32),
            pltpu.VMEM((nz, per, 8, LANES), F32),
            pltpu.VMEM((nz, per, 8, LANES), F32),
            pltpu.VMEM((groups * ny * nz * per, 8, LANES), F32),
            dma((2,)),
            dma((nz,)), dma((nz,)), dma((ny,)), dma((ny,)), dma((ny,)), dma((ny,)), dma, dma,
            dma((4,)), dma((4,)),
            dma, dma, dma, dma, dma, dma, dma,
            dma((groups, ny)),
            dma, dma,
        ],
        compiler_params=pltpu.CompilerParams(collective_id=0, has_side_effects=True),
        name="main",
    )(batch_index, exc_alpha, exc_beta.swapaxes(1, 2), one_body, civec)
    return tuple(pl.pallas_call(
        functools.partial(place_kernel, groups, shape, slots, pairs, total * width * parts),
        out_shape=(
            jax.ShapeDtypeStruct((batch, width), F32),
            jax.ShapeDtypeStruct((2, pairs), F32),
            jax.ShapeDtypeStruct((pairs, pairs), F32),
            jax.ShapeDtypeStruct((pairs, pairs), F32),
        ),
        in_specs=[vmem, vmem, vmem],
        out_specs=(vmem, vmem, vmem, vmem),
        scratch_shapes=[pltpu.VMEM((groups * ROWS, deep), F32)] * 2 + [pltpu.VMEM((groups, 8, LANES), F32)],
        name="place",
    )(exc_alpha, gat, sigma))


def solution(mesh, shape=(8, 4, 2)):
    in_specs = (P("alpha", "beta"), P(), P(), P(None, "beta", None), P())
    out_specs = (P("alpha", "beta"), P(), P(), P())
    return jax.shard_map(
        functools.partial(body, shape), mesh=mesh, in_specs=in_specs, out_specs=out_specs, check_vma=False
    )
```

```python
import functools
import math

import jax
import jax.numpy as jnp
from jax import lax
from jax.experimental import pallas as pl
from jax.experimental.pallas import tpu as pltpu
from jax.sharding import PartitionSpec as P

MESH = pl.DeviceIdType.MESH
F32, BF16, I32 = jnp.float32, jnp.bfloat16, jnp.int32
LANES = 128
HALF = 42
SHIFT = 68
ROWS = 168
EMPTY = 511
NT = (((1,), (1,)), ((), ()))
NN = (((1,), (0,)), ((), ()))
ALONG = lax.GatherDimensionNumbers(
    offset_dims=(), collapsed_slice_dims=(1,), start_index_map=(1,), operand_batching_dims=(0,), start_indices_batching_dims=(0,)
)


def split(x):
    high = x.astype(BF16)
    return high, (x - high.astype(F32)).astype(BF16)


def dot(a, b, dims):
    return lax.dot_general(a, b, dims, preferred_element_type=F32)


def dot3(a, b, dims):
    return dot(a[0], b[0], dims) + (dot(a[0], b[1], dims) + dot(a[1], b[0], dims))


def dot2(a, b, dims):
    return dot(a, b[0], dims) + dot(a, b[1], dims)


def lanes_of(x, index):
    return lax.gather(x, index[..., None], ALONG, (1, 1), mode=lax.GatherScatterMode.PROMISE_IN_BOUNDS)


def barrel(x, amount, bits):
    for bit in range(bits):
        moved = pltpu.roll(x, 1 << bit, 1)
        x = jnp.where(lax.rem(lax.div(amount, 1 << bit), 2) == 1, moved, x)
    return x


def packed_row(wide_ref, first, second, slots, end_first, end_second):
    string = slots + 1
    wide_ref[...] = jnp.zeros_like(wide_ref)
    wide_ref[0:1, 0:slots] = first
    wide_ref[1:2, 0:slots] = second
    lane = lax.broadcasted_iota(I32, (1, 2 * LANES), 1)
    blank = jnp.zeros((1, LANES), F32)
    one = jnp.concatenate([wide_ref[0:1, :], blank], axis=1)
    two = pltpu.roll(jnp.concatenate([wide_ref[1:2, :], blank], axis=1), string, 1)
    out = jnp.where(lane < string, one, two)
    out = jnp.where(lane == slots, end_first, jnp.where(lane == string + slots, end_second, out))
    return jnp.where(lane < 2 * string, out, float(EMPTY))


def main_kernel(groups, shape, slots, pairs, batch_ref, exc_ref, beta_hbm, h_ref, civ_hbm, sigma_ref, gat,
                beta_ref, civ_ref, pair_ref, look_ref, sign_ref, hx_ref, inv_ref, rows_s, table, texp, t_ref, vals_ref, blk_ref, line_ref,
                wide_ref, tiles_ref, pair_buf, sums, y_got, y_sum, got_ref, zbuf, dummy,
                in_sem, ts, tr, ys, yr, ws, wr, vs, vr, xs, xr, ps, pr, ssem, rsem, zs, zr, fs, fr, cs, cr):
    nz, ny, nc = shape
    parts = nz * ny * nc
    per = 64 // parts
    width = beta_ref.shape[2]
    cuts = width // LANES
    deep = 3 * LANES
    slots_deep = look_ref.shape[1]
    rows_dev = civ_ref.shape[0]
    string = slots + 1
    ga = lax.axis_index("alpha")
    me = lax.axis_index("beta")
    z, y, core = me // (ny * nc), (me // nc) % ny, me % nc
    planes = groups * ny

    def at(zz, yy, cc):
        return (zz * ny + yy) * nc + cc

    loads = [pltpu.make_async_copy(civ_hbm, civ_ref, in_sem.at[0]), pltpu.make_async_copy(beta_hbm, beta_ref, in_sem.at[1])]
    for load in loads:
        load.start()
    barrier = pltpu.get_barrier_semaphore()
    twin = at(z, y, 1 - core)
    z_far = sorted(range(1, nz), key=lambda k: -min(k, nz - k))
    y_far = sorted(range(1, ny), key=lambda k: -min(k, ny - k))
    for k in z_far:
        pl.semaphore_signal(barrier, inc=1, device_id=(ga, at(lax.rem(z + k, nz), y, core)), device_id_type=MESH)

    def spread_of(k):
        return min(k // ny, groups - k // ny) + min(k % ny, ny - k % ny)

    near = sorted(range(1, planes), key=spread_of)
    around = [(lax.rem(ga + k // ny, groups), lax.rem(y + k % ny, ny), k // ny) for k in near]
    for aa, yy, _ in around[::-1]:
        pl.semaphore_signal(barrier, inc=1, device_id=(aa, at(z, yy, core)), device_id_type=MESH)
    pl.semaphore_signal(barrier, inc=1, device_id=(ga, twin), device_id_type=MESH)
    for load in loads:
        load.wait()
    for b in range(2):
        row = civ_ref[pl.ds(lax.rem(batch_ref[2 * ga + b], rows_dev), 1), :]
        for t in range(cuts):
            rows_s[b * cuts + t : b * cuts + t + 1, :] = row[:, t * LANES : (t + 1) * LANES]

    last_tile = slots_deep - 8
    for lt in range(cuts):
        cut = slice(lt * LANES, (lt + 1) * LANES)
        pair_ref[lt, last_tile:, :] = jnp.full((8, LANES), EMPTY, I32)
        look_ref[lt, last_tile:, :] = jnp.zeros((8, LANES), I32)
        sign_ref[lt, last_tile:, :] = jnp.zeros((8, LANES), F32)
        look_ref[lt, 0:slots, :] = beta_ref[0, :, cut]
        pair_ref[lt, 0:slots, :] = beta_ref[1, :, cut]
        sign_ref[lt, 0:slots, :] = beta_ref[2, :, cut].astype(F32)

    blocks = [(lt, base) for base in range(0, pairs, LANES) for lt in range(cuts)]

    def invert(lt, base):
        size = min(LANES, -(-(pairs - base) // 8) * 8)
        ids = lax.broadcasted_iota(I32, (size, LANES), 0) + base

        def mark(e, acc):
            for k in range(9):
                acc = jnp.where(pair_ref[lt, pl.ds(9 * e + k, 1), :] == ids, 9 * e + k, acc)
            return acc

        acc = lax.fori_loop(0, slots // 9, mark, jnp.full((size, LANES), LANES - 1, I32))
        if size < LANES:
            acc = jnp.concatenate([acc, jnp.full((LANES - size, LANES), LANES - 1, I32)], axis=0)
        inv_ref[lt * LANES : (lt + 1) * LANES, base : base + LANES] = acc.T

    early = 2
    for block in blocks[:early]:
        invert(*block)

    pl.semaphore_wait(barrier, nz - 1 + planes - 1 + 1)

    def row_copy(to_z, slot_z):
        return pltpu.make_async_remote_copy(
            rows_s, table.at[y, core, slot_z], ts.at[to_z], tr.at[slot_z],
            device_id=(ga, at(to_z, y, core)), device_id_type=MESH,
        )

    def line_copy(to_y, slot_y):
        return pltpu.make_async_remote_copy(
            table.at[y, core], table.at[slot_y, core], ys.at[to_y], yr.at[slot_y],
            device_id=(ga, at(z, to_y, core)), device_id_type=MESH,
        )

    def twin_line(slot_y, slot_c):
        return pltpu.make_async_remote_copy(
            table.at[slot_y, core], table.at[slot_y, slot_c], ws.at[slot_y], wr.at[slot_y],
            device_id=(ga, twin), device_id_type=MESH,
        )

    for k in z_far:
        row_copy(lax.rem(z + k, nz), z).start()

    right, left = lax.rem(ga + 1, groups), lax.rem(ga + groups - 1, groups)
    half_rows = rows_dev // 2

    def block_copy(src, dst, k, to):
        return pltpu.make_async_remote_copy(
            src, dst, xs.at[k], xr.at[k], device_id=(to, me), device_id_type=MESH
        )

    first_half, second_half = pl.ds(0, half_rows), pl.ds(half_rows, half_rows)
    hops = [
        block_copy(civ_ref, blk_ref.at[0], 0, right),
        block_copy(civ_ref, blk_ref.at[1], 1, left),
        block_copy(blk_ref.at[0, first_half], blk_ref.at[2, first_half], 2, right),
        block_copy(blk_ref.at[1, second_half], blk_ref.at[2, second_half], 3, left),
    ]
    if groups == 2:
        hops = hops[:1]
    for hop in hops[:2]:
        hop.start()
    table[y, core, z] = rows_s[...]

    for block in blocks[early:]:
        invert(*block)

    line_ref[...] = jnp.zeros_like(line_ref)
    line_ref[0:1, 0:pairs] = h_ref[...].reshape(1, pairs)
    strips = [jnp.broadcast_to(line_ref[0:1, k * LANES : (k + 1) * LANES], (8, LANES)) for k in range(3)]

    def h_of(index):
        low = jnp.bitwise_and(index, 127)
        high = lax.shift_right_logical(index, 7)
        out = jnp.zeros(index.shape, F32)
        for k in range(3):
            out = jnp.where(high == k, lanes_of(strips[k], low), out)
        return out

    def h_step(i, c):
        start = pl.multiple_of(8 * i, 8)
        for lt in range(cuts):
            hx_ref[lt, pl.ds(start, 8), :] = h_of(pair_ref[lt, pl.ds(start, 8), :])
        return c

    lax.fori_loop(0, slots_deep // 8, h_step, 0)

    s_row = packed_row(
        wide_ref, exc_ref[0, pl.ds(2 * ga, 1), :].astype(F32), exc_ref[0, pl.ds(2 * ga + 1, 1), :].astype(F32), slots,
        batch_ref[2 * ga].astype(F32), batch_ref[2 * ga + 1].astype(F32),
    )
    g_row = packed_row(
        wide_ref, exc_ref[2, pl.ds(2 * ga, 1), :].astype(F32), exc_ref[2, pl.ds(2 * ga + 1, 1), :].astype(F32), slots, 1.0, 1.0
    )
    p_row = packed_row(
        wide_ref, exc_ref[1, pl.ds(2 * ga, 1), :].astype(F32), exc_ref[1, pl.ds(2 * ga + 1, 1), :].astype(F32), slots,
        float(EMPTY), float(EMPTY),
    )
    wide_lane = lax.broadcasted_iota(I32, (1, 2 * LANES), 1)
    g_row = jnp.where(wide_lane < 2 * string, g_row, 0.0)
    h_row = jnp.concatenate(
        [h_of(jnp.broadcast_to(p_row[:, k : k + LANES], (8, LANES)).astype(I32))[0:1] for k in (0, LANES)], axis=1
    )
    meta = jnp.concatenate(
        [s_row, g_row, jnp.where(wide_lane < string, h_row, 0.0), jnp.where(wide_lane < string, 0.0, h_row),
         jnp.zeros((4, 2 * LANES), F32)], axis=0
    ).T[0:ROWS]
    source, sign = meta[:, 0:1], meta[:, 1:2]

    def choose(block, owner):
        ids = (lax.broadcasted_iota(I32, (ROWS, rows_dev), 1) + owner * rows_dev).astype(F32)
        pick = jnp.where(source == ids, sign, 0.0).astype(BF16)
        parts2 = split(block)
        return dot(pick, parts2[0], NN), dot(pick, parts2[1], NN)

    a_high, a_low = choose(civ_ref[...], ga)

    def arrive(yy, cc):
        def step(zz, c):
            for b in range(2):
                for t in range(cuts):
                    line = table[yy, cc, zz, b * cuts + t : b * cuts + t + 1, :]
                    spot = cuts * at(zz, yy, cc) + t
                    texp[b, spot] = jnp.broadcast_to(line, (8, LANES))
                    t_ref[b, pl.ds(spot, 1), :] = line
            return c

        lax.fori_loop(0, nz, step, 0)

    for k in z_far[::-1]:
        zz = lax.rem(z + k, nz)
        row_copy(zz, zz).wait_recv()
    for k in y_far:
        line_copy(lax.rem(y + k, ny), y).start()
    twin_line(y, core).start()
    arrive(y, core)
    for k in y_far[::-1]:
        yy = lax.rem(y + k, ny)
        line_copy(yy, yy).wait_recv()
        twin_line(yy, core).start()
        arrive(yy, core)
    for k in [0] + y_far[::-1]:
        yy = lax.rem(y + k, ny)
        twin_line(yy, 1 - core).wait_recv()
        arrive(yy, 1 - core)

    total_rows = parts * cuts
    chunk = 24
    halves = split(jnp.concatenate([t_ref[0], t_ref[1]], axis=0))
    full = jnp.concatenate(halves, axis=1)

    levels = 3 if total_rows % 64 == 0 else 0

    def mux(got, high, low_bit, count):
        for bit in range(low_bit, low_bit + count):
            n = got.shape[0] // 2
            got = got.reshape(n, 2, 8, LANES)
            mask = jnp.broadcast_to(jnp.bitwise_and(high, 1 << bit)[None], (n, 8, LANES)) != 0
            got = jnp.where(mask, got[:, 1], got[:, 0])
        return got

    sub = lax.broadcasted_iota(I32, (8, LANES), 0)
    tall = lax.broadcasted_iota(I32, (LANES, LANES), 0).astype(F32).astype(BF16)
    blank_hot, full_hot = jnp.zeros((LANES, LANES), BF16), jnp.ones((LANES, LANES), BF16)

    def match(lines):
        hot = []
        for low, _ in lines:
            line = jnp.broadcast_to(low, (16, LANES)).astype(F32).astype(BF16)
            hot.append(jnp.where(tall == jnp.concatenate([line] * 8, axis=0), full_hot, blank_hot))
        hot = jnp.concatenate(hot, axis=1) if len(hot) > 1 else hot[0]
        found = dot(full, jnp.concatenate([hot, hot], axis=0), NN)
        values = []
        for k, (_, high) in enumerate(lines):
            wide = jnp.broadcast_to(high, (8, LANES))
            near = jnp.bitwise_and(wide, 7) == sub
            block = lax.shift_right_logical(wide, 3 + levels)
            both = []
            for b in range(2):
                mine = found[b * total_rows : (b + 1) * total_rows, k * LANES : (k + 1) * LANES]
                mine = mux(mine.reshape(total_rows // 8, 8, LANES), wide, 3, levels)
                best = mine[0]
                for q in range(1, mine.shape[0]):
                    best = jnp.where(block == q, mine[q], best)
                both.append(jnp.sum(jnp.where(near, best, 0.0), axis=0, keepdims=True))
            values.append(both)
        return values

    def look_up(i, live):
        start = pl.multiple_of(8 * i, 8)
        low, high, acc = [], [], []
        for lt in range(cuts):
            src = look_ref[lt, pl.ds(start, 8), :]
            low.append(jnp.bitwise_and(src, 127))
            high.append(lax.shift_right_logical(src, 7))
            acc.append([jnp.zeros((8, LANES), F32)] * 2)
        direct = 1 if live == 8 else 0
        if direct:
            group = lax.shift_right_logical(high[0], 3)
            index = jnp.broadcast_to(low[0][None], (chunk, 8, LANES)).reshape(chunk * 8, LANES)
            for base in range(0, total_rows, chunk):
                for b in range(2):
                    got = texp[b, base : base + chunk].reshape(chunk * 8, LANES)
                    got = mux(lanes_of(got, index).reshape(chunk, 8, LANES), high[0], 0, 3)
                    for k in range(chunk // 8):
                        acc[0][b] = jnp.where(group == base // 8 + k, got[k], acc[0][b])
        spots = [(lt, r) for lt in range(direct, cuts) for r in range(live)]
        for n in range(0, len(spots), 2):
            some = spots[n : n + 2]
            values = match([(low[lt][r : r + 1], high[lt][r : r + 1]) for lt, r in some])
            for (lt, r), both in zip(some, values):
                for b in range(2):
                    acc[lt][b] = jnp.where(sub == r, both[b], acc[lt][b])
        for lt in range(cuts):
            factor = sign_ref[lt, pl.ds(start, 8), :]
            for b in range(2):
                vals_ref[b, lt, pl.ds(start, 8), :] = acc[lt][b] * factor

    def look_two(i, c):
        look_up(2 * i, 8)
        look_up(2 * i + 1, 8)
        return c

    tiles = slots_deep // 8
    relay = tiles // 4
    lax.fori_loop(0, relay, look_two, 0)
    for hop in hops[:2]:
        hop.wait_recv()
    for hop in hops[2:]:
        hop.start()
    lax.fori_loop(relay, tiles // 2, look_two, 0)
    for i in range(tiles // 2 * 2, tiles):
        look_up(i, min(8, slots - 8 * i))
    for hop in hops[2:]:
        hop.wait_recv()

    blank = jnp.zeros((LANES - slots_deep, LANES), F32)
    d2 = []
    for b in range(2):
        by_slot = jnp.concatenate(
            [jnp.concatenate([vals_ref[b, lt], blank], axis=0).T for lt in range(cuts)], axis=0
        )
        d2.append(split(jnp.concatenate(
            [lanes_of(by_slot, inv_ref[:, base : base + LANES]) for base in range(0, deep, LANES)], axis=1
        )))

    owners = [lax.rem(ga + groups - 1, groups), lax.rem(ga + 1, groups), lax.rem(ga + 2, groups)]
    for k in range(groups - 1):
        more = choose(blk_ref[k], owners[k])
        a_high, a_low = a_high + more[0], a_low + more[1]
    a2 = (a_high.astype(BF16), a_low.astype(BF16))
    a = a_high + a_low

    def times(left, right, dims):
        n = left[0].shape[0]
        both = dot(jnp.concatenate(left, axis=0), right[0], dims)
        return (both[:n] + both[n:]) + dot(left[0], right[1], dims)

    row = lax.broadcasted_iota(I32, (ROWS, 1), 0)
    first = row < string
    low_rows, high_rows = 96, 80
    m0 = times(tuple(p[:low_rows] for p in a2), d2[0], NN)
    m1 = times(tuple(p[high_rows:] for p in a2), d2[1], NN)
    m = jnp.where(
        first,
        jnp.concatenate([m0, jnp.zeros((ROWS - low_rows, deep), F32)], axis=0),
        jnp.concatenate([jnp.zeros((high_rows, deep), F32), m1], axis=0),
    )
    gram = times(a2, a2, NT)
    gram = jnp.concatenate([gram, jnp.zeros((ROWS, 2 * LANES - ROWS), F32)], axis=1)
    gram = jnp.where(first, gram, pltpu.roll(gram, 2 * LANES - string, 1))
    again = pltpu.roll(gram, string, 1)[:, 0:LANES]
    lane = lax.broadcasted_iota(I32, (ROWS, LANES), 1)
    gram = jnp.where(lane < string, gram[:, 0:LANES], again)
    local = jnp.where(first, row, row - string)
    folded = barrel(gram, lax.rem(SHIFT - local + 2 * LANES, LANES), 7)
    last = jnp.where(lane < SHIFT, m[:, 2 * LANES :], jnp.where(lane < SHIFT + HALF, folded, 0.0))
    for rg in range(ROWS // 8):
        for lt in range(3):
            k = rg * 3 + lt
            piece = last if lt == 2 else m[:, lt * LANES : (lt + 1) * LANES]
            tiles_ref[(k // per) % nc, k // per // nc, k % per] = piece[8 * rg : 8 * rg + 8]
    tiles_ref[nc - 1, parts // nc - 1, per - 1] = jnp.zeros((8, LANES), F32)

    def settled(count, sem):
        return pltpu.make_async_remote_copy(
            dummy.at[pl.ds(0, count)], dummy.at[pl.ds(0, count)], sem, sem, device_id=(right, me), device_id_type=MESH
        )

    chips = parts // nc
    chip = z * ny + y
    def pair_copy(yy):
        rows = pl.ds(yy * nz, nz)
        return pltpu.make_async_remote_copy(
            tiles_ref.at[1 - core, rows], pair_buf.at[rows], ps.at[yy], pr.at[yy],
            device_id=(ga, twin), device_id_type=MESH,
        )

    turns = [lax.rem(y + k, ny) for k in y_far] + [y]
    for yy in turns:
        pair_copy(yy).start()

    def y_part(yy):
        return pltpu.make_async_remote_copy(
            sums.at[pl.ds(yy * nz, nz)], y_got.at[y], ssem, rsem, device_id=(ga, at(z, yy, core)), device_id_type=MESH
        )

    for k, yy in enumerate(turns):
        rows = pl.ds(yy * nz, nz)
        pair_copy(yy).wait_recv()
        part = tiles_ref[core, rows] + pair_buf[rows]
        if k < len(y_far):
            sums[rows] = part
            y_part(yy).start()
        else:
            y_got[y] = part
    for k in z_far:
        row_copy(lax.rem(z + k, nz), z).wait_send()
    for k in y_far:
        line_copy(lax.rem(y + k, ny), y).wait_send()
    for yy in range(ny):
        twin_line(yy, core).wait_send()
    for hop in hops:
        hop.wait_send()
    for yy in range(ny):
        pair_copy(yy).wait_send()
    for b in range(2):
        from_a = jnp.sum(a * meta[:, 2 + b : 3 + b], axis=0, keepdims=True)
        for lt in range(cuts):
            cut = slice(lt * LANES, (lt + 1) * LANES)
            from_b = jnp.sum(vals_ref[b, lt] * hx_ref[lt], axis=0, keepdims=True)
            sigma_ref[b : b + 1, cut] = from_a[:, cut] + from_b
    if ny > 1:
        settled((ny - 1) * nz * per, rsem).wait_recv()
    y_sum[...] = jnp.sum(y_got[...], axis=0)

    def z_part(zz):
        return pltpu.make_async_remote_copy(
            y_sum.at[zz], got_ref.at[z], vs, vr, device_id=(ga, at(zz, y, core)), device_id_type=MESH
        )

    for k in z_far:
        z_part(lax.rem(z + k, nz)).start()
    got_ref[z] = y_sum[z]
    if ny > 1:
        settled((ny - 1) * nz * per, ssem).wait_send()
    if nz > 1:
        settled((nz - 1) * per, vr).wait_recv()
    zbuf[z] = jnp.sum(got_ref[...], axis=0)

    def z_copy(zz):
        return pltpu.make_async_remote_copy(
            zbuf.at[z], zbuf.at[z], zs, zr, device_id=(ga, at(zz, y, core)), device_id_type=MESH
        )

    for k in sorted(range(1, nz), key=lambda k: -min(k, nz - k)):
        z_copy(lax.rem(z + k, nz)).start()
    if nz > 1:
        settled((nz - 1) * per, vs).wait_send()
    if nz > 1:
        settled((nz - 1) * per, zr).wait_recv()

    def plane_copy(src, aa, yy, slot_a, slot_y):
        return pltpu.make_async_remote_copy(
            src, gat.at[slot_a, slot_y, core], fs, fr.at[slot_a, slot_y],
            device_id=(aa, at(z, yy, core)), device_id_type=MESH,
        )

    def twin_copy(src, slot_a, slot_y):
        return pltpu.make_async_remote_copy(
            src, gat.at[slot_a, slot_y, core], cs, cr,
            device_id=(ga, at(z, y, 1 - core)), device_id_type=MESH,
        )

    for aa, yy, _ in around[::-1]:
        plane_copy(zbuf, aa, yy, ga, y).start()
    twin_copy(zbuf, ga, y).start()
    gat[ga, y, core] = zbuf[...]
    for aa, yy, _ in around:
        plane_copy(zbuf, aa, yy, aa, yy).wait_recv()
        twin_copy(gat.at[aa, yy, core], aa, yy).start()
    if nz > 1:
        settled((nz - 1) * per, zs).wait_send()
    settled((planes - 1) * nz * per, fs).wait_send()
    settled(planes * nz * per, cr).wait_recv()
    settled(planes * nz * per, cs).wait_send()


def place_kernel(groups, shape, slots, pairs, norm, exc_ref, gat, sigma_in, sigma_ref, density_ref, same_ref, mixed_ref,
                 r_ref, t_ref, wide_ref):
    nz, ny, nc = shape
    per = 64 // (nz * ny * nc)
    string = slots + 1
    deep = 3 * LANES
    sigma_ref[...] = sigma_in[...]
    row = lax.broadcasted_iota(I32, (ROWS, 1), 0)
    first = row < string
    local = jnp.where(first, row, row - string)
    amount = lax.rem(local - SHIFT + 2 * LANES, LANES)
    lane = lax.broadcasted_iota(I32, (ROWS, LANES), 1)
    weights = jnp.where((lane == SHIFT) | (lane == SHIFT + HALF - 1), 0.5, 1.0)
    weights = jnp.where((lane >= SHIFT) & (lane < SHIFT + HALF), weights, 0.0)
    strip = lax.broadcasted_iota(I32, (1, LANES), 1)
    wide = lax.broadcasted_iota(I32, (1, 2 * LANES), 1)
    span = -(-groups * ROWS // LANES) * LANES
    p_all = jnp.zeros((1, span), F32)
    exts = []
    for g in range(groups):
        rows = slice(g * ROWS, (g + 1) * ROWS)
        for rg in range(ROWS // 8):
            for lt in range(3):
                k = rg * 3 + lt
                j, s = k // per, k % per
                r_ref[g * ROWS + 8 * rg : g * ROWS + 8 * rg + 8, lt * LANES : (lt + 1) * LANES] = gat[
                    g, j // nc // nz, j % nc, (j // nc) % nz, s
                ]
        ids = exc_ref[1, 2 * g : 2 * g + 2, :].astype(F32)
        p_row = packed_row(wide_ref.at[g], ids[0:1], ids[1:2], slots, float(pairs), float(pairs))
        p_row = jnp.where(wide < ROWS, p_row, 0.0)
        p_row = jnp.concatenate([p_row, jnp.zeros((1, span - 2 * LANES), F32)], axis=1)
        p_all = p_all + (pltpu.roll(p_row, g * ROWS, 1) if g else p_row)
        ends = []
        for b in range(2):
            line = wide_ref[g, b : b + 1, :]
            again = pltpu.roll(line, string, 1)
            line = jnp.where(strip < slots, line, jnp.where(strip == slots, float(pairs), again))
            ends.append(line)
        exts.append(jnp.concatenate(ends, axis=1))
    exts = jnp.concatenate(exts + [jnp.zeros((8 - groups, 2 * LANES), F32)], axis=0).T
    for g in range(groups):
        rows = slice(g * ROWS, (g + 1) * ROWS)
        half = barrel(r_ref[rows, 2 * LANES :] * weights, amount, 7)
        both = split(jnp.concatenate([jnp.where(first, half, 0.0), jnp.where(first, 0.0, half)], axis=1))
        right = (lax.broadcasted_iota(I32, (2 * LANES, deep), 1).astype(F32) == exts[:, g : g + 1]).astype(BF16)
        twice = dot(jnp.concatenate(both, axis=0), right, NN)
        t_ref[rows, :] = twice[:ROWS] + twice[ROWS:]
    tall = -(-(pairs + 1) // 8) * 8
    placing = (lax.broadcasted_iota(I32, (tall, groups * ROWS), 0).astype(F32) == p_all[:, : groups * ROWS]).astype(BF16)
    placed = dot2(placing, split(jnp.concatenate([r_ref[...], t_ref[...]], axis=1)), NN)
    mixed = placed[:, :deep]
    upper = jnp.concatenate([placed[:, deep:], jnp.zeros((deep - tall, deep), F32)], axis=0)
    root = math.sqrt(norm)
    same = upper + upper.T
    density_ref[0:1, :] = same[pairs : pairs + 1, 0:pairs] * (1.0 / root)
    density_ref[1:2, :] = mixed[pairs : pairs + 1, 0:pairs] * (1.0 / root)
    same_ref[...] = same[0:pairs, 0:pairs] * (1.0 / norm)
    mixed_ref[...] = mixed[0:pairs, 0:pairs] * (1.0 / root)


def body(shape, civec, batch_index, exc_alpha, exc_beta, one_body):
    vmem = pl.BlockSpec(memory_space=pltpu.VMEM)
    smem = pl.BlockSpec(memory_space=pltpu.SMEM)
    anywhere = pl.BlockSpec(memory_space=pl.ANY)
    nz, ny, nc = shape
    parts = nz * ny * nc
    per = 64 // parts
    groups = lax.axis_size("alpha")
    rows_dev, width = civec.shape
    total = batch_index.shape[0]
    batch = total // groups
    slots = exc_alpha.shape[2]
    pairs = one_body.shape[0]
    deep = 3 * LANES
    cuts = width // LANES
    slots_deep = -(-slots // 8) * 8
    dma = pltpu.SemaphoreType.DMA
    sigma, gat = pl.pallas_call(
        functools.partial(main_kernel, groups, shape, slots, pairs),
        out_shape=(
            jax.ShapeDtypeStruct((batch, width), F32),
            jax.ShapeDtypeStruct((groups, ny, nc, nz, per, 8, LANES), F32),
        ),
        in_specs=[smem, vmem, anywhere, vmem, anywhere],
        out_specs=(vmem, vmem),
        scratch_shapes=[
            pltpu.VMEM((3, slots, width), I32),
            pltpu.VMEM((rows_dev, width), F32),
            pltpu.VMEM((cuts, slots_deep, LANES), I32),
            pltpu.VMEM((cuts, slots_deep, LANES), I32),
            pltpu.VMEM((cuts, slots_deep, LANES), F32),
            pltpu.VMEM((cuts, slots_deep, LANES), F32),
            pltpu.VMEM((width, deep), I32),
            pltpu.VMEM((2 * cuts, LANES), F32),
            pltpu.VMEM((ny, nc, nz, 2 * cuts, LANES), F32),
            pltpu.VMEM((2, parts * cuts, 8, LANES), F32),
            pltpu.VMEM((2, parts * cuts, LANES), F32),
            pltpu.VMEM((2, cuts, slots_deep, LANES), F32),
            pltpu.VMEM((max(groups - 1, 2), rows_dev, width), F32),
            pltpu.VMEM((8, deep), F32),
            pltpu.VMEM((8, LANES), F32),
            pltpu.VMEM((nc, parts // nc, per, 8, LANES), F32),
            pltpu.VMEM((parts // nc, per, 8, LANES), F32),
            pltpu.VMEM((parts // nc, per, 8, LANES), F32),
            pltpu.VMEM((ny, nz, per, 8, LANES), F32),
            pltpu.VMEM((nz, per, 8, LANES), F32),
            pltpu.VMEM((nz, per, 8, LANES), F32),
            pltpu.VMEM((nz, per, 8, LANES), F32),
            pltpu.VMEM((groups * ny * nz * per, 8, LANES), F32),
            dma((2,)),
            dma((nz,)), dma((nz,)), dma((ny,)), dma((ny,)), dma((ny,)), dma((ny,)), dma, dma,
            dma((4,)), dma((4,)),
            dma((ny,)), dma((ny,)), dma, dma, dma, dma, dma,
            dma((groups, ny)),
            dma, dma,
        ],
        compiler_params=pltpu.CompilerParams(collective_id=0, has_side_effects=True),
        name="main",
    )(batch_index, exc_alpha, exc_beta.swapaxes(1, 2), one_body, civec)
    return tuple(pl.pallas_call(
        functools.partial(place_kernel, groups, shape, slots, pairs, total * width * parts),
        out_shape=(
            jax.ShapeDtypeStruct((batch, width), F32),
            jax.ShapeDtypeStruct((2, pairs), F32),
            jax.ShapeDtypeStruct((pairs, pairs), F32),
            jax.ShapeDtypeStruct((pairs, pairs), F32),
        ),
        in_specs=[vmem, vmem, vmem],
        out_specs=(vmem, vmem, vmem, vmem),
        scratch_shapes=[pltpu.VMEM((groups * ROWS, deep), F32)] * 2 + [pltpu.VMEM((groups, 8, LANES), F32)],
        name="place",
    )(exc_alpha, gat, sigma))


def solution(mesh, shape=(8, 4, 2)):
    in_specs = (P("alpha", "beta"), P(), P(), P(None, "beta", None), P())
    out_specs = (P("alpha", "beta"), P(), P(), P())
    return jax.shard_map(
        functools.partial(body, shape), mesh=mesh, in_specs=in_specs, out_specs=out_specs, check_vma=False
    )
```
